128 devices in a mesh: item: 4 (over x), row: 16 (over z, y), col: 2 (over core).
Axes of the slice: x: 4, y: 4, z: 4, core: 2. Of those that a mesh axis runs over, the one named last changes fastest.
Arguments:
- img_hidden: bfloat16 [32, 1024, 3072], P('item', ('row', 'col')), parts along dimension 0, may hold values from -1.796875 to 1.796875
- text_hidden: bfloat16 [32, 512, 3072], P('item', ('row', 'col')), parts along dimension 0, may hold values from -1.796875 to 1.796875
- latent: float32 [32, 1024, 64], P('item', ('row', 'col')), parts along dimension 0, may hold values from -6 to 6
- text_len: int32 [32], P('item'), parts along dimension 0, may hold values from 1 to 512, as said below
- block_keep: int32 [32, 16], P('item'), parts along dimension 0, may hold values 0 or 1
- img_pos: int32 [1024, 3], P(('row', 'col')), may hold values from 0 to 62, as said below
- modulation: float32 [32, 5, 3072], P('item'), parts along dimension 0, may hold values from -4 to 4
- qk_gain: float32 [2, 128], replicated, may hold values from 0.7 to 7
- w_qkv: bfloat16 [3072, 3, 1536], P(None, None, 'col'), may hold values from -0.109375 to 0.109375
- w_out: bfloat16 [1536, 3072], P('col'), may hold values from -0.25 to 0.25
- w_final: bfloat16 [3072, 64], replicated, may hold values from -0.109375 to 0.109375
Outputs:
- img_out: bfloat16 [32, 1024, 3072], P('item', ('row', 'col')), parts along dimension 0
- text_out: bfloat16 [32, 512, 3072], P('item', ('row', 'col')), parts along dimension 0
- latent_next: float32 [32, 1024, 64], P('item', ('row', 'col')), parts along dimension 0
The draws below stay inside these ranges and needn't reach their ends.
There are 4 independent parts, one for each index of `item`. The reference program is written for one: setup_inputs(seed, part) draws one part's arguments, and reference() takes and returns one part's arrays. A program takes and returns all parts, laid end to end along the dimension named above; an argument that names none is the same for every part. Nothing has to cross between parts.
Inputs may be any that keep to these rules, and one draw needn't show every extreme that they name: `text_len`: at least one sample of every request uses all 512 text slots. `img_pos`: image token i, in image row r = i // 32 and column q = i % 32, has ids (c_i, a_r + r, b_q + q), where every token has its own frame id c_i of 0 to 3, every image row its own offset a_r and every image column its own offset b_q, each of 0 to 31.
All inputs are finite; a program needn't handle non-finite values.
Results may differ from the reference program's by a relative error of at most 0.015.
The reference program's roundings to bfloat16 on the way count: a program that leaves them out, or rounds other values in their place, can miss the bound.
Values may be sent and summed in bfloat16 or wider, within the bound.
No kernel may reach another device: no remote copies, remote signals or barrier semaphores. Data moves between devices by JAX's collectives and lax.ppermute only.
A program may use at most 256 MiB of HBM per device.

```python
import jax
import jax.numpy as jnp
import numpy as np
from jax import lax

D = 3072
HEADS = 12
HD = 128
LAT = 64
SIDE = 32
TXT = 512
KBLK = 64
SAMPLES = 8
IMG = 1024
IMG_BLOCKS = 16


def draw_text_len(key, part):
    first_key, second_key = jax.random.split(key)
    lengths = jax.random.randint(first_key, (SAMPLES,), 1, TXT + 1)
    chosen = jax.random.randint(second_key, (), 0, SAMPLES)
    return jnp.where(jnp.arange(SAMPLES) == chosen, TXT, lengths).astype(jnp.int32)


def draw_img_pos(key, part):
    frame_key, row_key, col_key = jax.random.split(key, 3)
    frames = jax.random.randint(frame_key, (IMG,), 0, 4).astype(jnp.int32)
    line = jnp.arange(SIDE, dtype=jnp.int32)
    row_offsets = jax.random.randint(row_key, (SIDE,), 0, SIDE).astype(jnp.int32)
    row_offsets = jnp.where(line == 0, 0, row_offsets)
    row_offsets = jnp.where(line == SIDE - 1, SIDE - 1, row_offsets)
    col_offsets = jax.random.randint(col_key, (SIDE,), 0, SIDE).astype(jnp.int32)
    index = jnp.arange(IMG, dtype=jnp.int32)
    image_row = index // SIDE
    image_col = index % SIDE
    row_onehot = (image_row[:, None] == line[None, :]).astype(jnp.int32)
    col_onehot = (image_col[:, None] == line[None, :]).astype(jnp.int32)
    row_ids = image_row + jnp.sum(row_onehot * row_offsets[None, :], axis=1)
    col_ids = image_col + jnp.sum(col_onehot * col_offsets[None, :], axis=1)
    return jnp.stack([frames, row_ids, col_ids], axis=1).astype(jnp.int32)


def draw_qk_gain(key, part):
    return jax.random.uniform(key, (2, HD), jnp.float32, 0.7, 1.4)


def set_ends(result, stream_key, low, largest):
    index_at = [jax.random.randint(jax.random.fold_in(stream_key, axis), (), 0, length) for axis, length in enumerate(result.shape)]
    main_axis = result.shape.index(max(result.shape))
    beside = index_at[:main_axis] + [(index_at[main_axis] + 1) % result.shape[main_axis]] + index_at[main_axis + 1:]
    return result.at[tuple(index_at)].set(low).at[tuple(beside)].set(largest)


def block_scale(key, dims, cuts, low, top_value):
    factor_of, own = 1.0, jax.random.fold_in(key, 6)
    for position, shards_of in cuts:
        draws = jnp.exp(jax.random.uniform(jax.random.fold_in(own, position), (shards_of,), jnp.float32, low / len(cuts), top_value / len(cuts)))
        factor_of = factor_of * jnp.repeat(draws, dims[position] // shards_of).reshape([-1 if axis == position else 1 for axis in range(len(dims))])
    return factor_of


def normal_values(rng, extent, scale, bound, shards=(), kind=jnp.bfloat16):
    values = scale * jax.random.normal(rng, extent, jnp.float32)
    if shards:
        values = values * block_scale(rng, extent, shards, -0.22, 0.18)
    return jnp.clip(values, -bound, bound).astype(kind)


def setup_inputs(seed: int = 0, part: int = 0) -> dict:
    seeds = jax.random.split(jax.random.key(seed), 12)
    own_keys = jax.random.split(jax.random.fold_in(seeds[11], part), 12)
    return {
        "img_hidden": normal_values(own_keys[0], (SAMPLES, IMG, D), 0.3, 1.796875, ((1, 32),)),
        "text_hidden": normal_values(own_keys[1], (SAMPLES, TXT, D), 0.3, 1.796875, ((1, 32),)),
        "latent": normal_values(own_keys[2], (SAMPLES, IMG, LAT), 1.0, 6.0, ((1, 32),), jnp.float32),
        "text_len": draw_text_len(jax.random.fold_in(jax.random.fold_in(seeds[11], part), 71), part),
        "block_keep": set_ends((jax.random.randint(own_keys[4], (SAMPLES, IMG_BLOCKS), 0, 4) < 3).astype(jnp.int32), jax.random.fold_in(own_keys[4], 1), 0, 1),
        "img_pos": draw_img_pos(jax.random.fold_in(seeds[11], 71), part),
        "modulation": normal_values(own_keys[6], (SAMPLES, 5, D), 1.0, 4.0, (), jnp.float32),
        "qk_gain": draw_qk_gain(jax.random.fold_in(seeds[11], 71), part),
        "w_qkv": normal_values(seeds[8], (D, 3, HEADS * HD), D ** -0.5, 0.109375, ((2, 2),)),
        "w_out": normal_values(seeds[9], (HEADS * HD, D), (4 * HD) ** -0.5, 0.25, ((0, 2),)),
        "w_final": normal_values(seeds[10], (D, LAT), D ** -0.5, 0.109375),
    }


eps_norm = 1e-06
theta_base = 10000.0
step_size = -0.25

def layer_norm(values):
    center = values - lax.optimization_barrier(jnp.mean(values, axis=-1, keepdims=True))
    return center * lax.rsqrt(lax.optimization_barrier(jnp.mean(center * center, axis=-1, keepdims=True)) + eps_norm)

def modulate(hidden, shift, scale):
    return ((1.0 + scale) * layer_norm(hidden.astype(jnp.float32)) + shift).astype(jnp.bfloat16)

def rope_tables(head_dim):
    half = head_dim // 2
    first = head_dim // 16
    second = (half - first) // 2
    counts = [first, second, half - first - second]
    tables = []
    for axis_id in range(3):
        pieces = []
        for other in range(3):
            if other == axis_id:
                pieces.append(theta_base ** (-np.arange(counts[other]) / counts[other]))
            else:
                pieces.append(np.zeros(counts[other]))
        tables.append(np.concatenate(pieces).astype(np.float32))
    return tables

def angles_of(positions, head_dim):
    tables = rope_tables(head_dim)
    angle = positions[:, 0:1] * jnp.asarray(tables[0]) + positions[:, 1:2] * jnp.asarray(tables[1])
    angle = angle + positions[:, 2:3] * jnp.asarray(tables[2])
    return (jnp.cos(angle), jnp.sin(angle))

def rotate(values, cosine, sine):
    half = values.shape[-1] // 2
    first_half = values[..., :half]
    second_half = values[..., half:]
    cos_rows = cosine[:, None, :]
    sin_rows = sine[:, None, :]
    return jnp.concatenate([first_half * cos_rows - second_half * sin_rows, second_half * cos_rows + first_half * sin_rows], axis=-1)

def rms_gain(values, gain):
    return values * lax.rsqrt(lax.optimization_barrier(jnp.mean(values * values, axis=-1, keepdims=True)) + eps_norm) * gain

def key_valid(text_len, block_keep, seq_len):
    index = jnp.arange(seq_len, dtype=jnp.int32)
    text_ok = index[None, :] < text_len[:, None]
    block_id = jnp.clip(index - TXT, 0, IMG - 1) // KBLK
    onehot = (block_id[:, None] == jnp.arange(IMG // KBLK, dtype=jnp.int32)[None, :]).astype(jnp.int32)
    img_ok = lax.optimization_barrier(jnp.sum(block_keep[:, None, :] * onehot[None], axis=-1)) > 0
    return jnp.where(index[None, :] < TXT, text_ok, img_ok)

def attend(operands):
    query, keys, values, valid = operands
    scores = jnp.einsum('qhd,khd->hqk', query.astype(jnp.float32), keys.astype(jnp.float32)) * HD ** (-0.5)
    scores = jnp.where(valid[None, None, :], scores, -jnp.inf)
    top = lax.optimization_barrier(jnp.max(scores, axis=-1, keepdims=True))
    weights = jnp.exp(scores - top)
    total = lax.optimization_barrier(jnp.sum(weights, axis=-1))
    rounded = lax.optimization_barrier(weights.astype(jnp.bfloat16)).astype(jnp.float32)
    summed = jnp.einsum('hqk,khd->qhd', rounded, values.astype(jnp.float32))
    return (summed / jnp.transpose(total)[:, :, None]).astype(jnp.bfloat16)

def reference(img_hidden, text_hidden, latent, text_len, block_keep, img_pos, modulation, qk_gain, w_qkv, w_out, w_final):
    samples = img_hidden.shape[0]
    width = img_hidden.shape[2]
    inner = w_out.shape[0]
    heads = inner // HD
    seq_len = TXT + IMG
    tokens = jnp.concatenate([text_hidden, img_hidden], axis=1)
    mod_rows = modulation[:, :, None, :]
    normed = modulate(tokens, mod_rows[:, 0], mod_rows[:, 1])
    mixed = jnp.dot(normed.reshape(samples * seq_len, width), w_qkv.reshape(width, 3 * inner), preferred_element_type=jnp.float32)
    mixed = mixed.reshape(samples, seq_len, 3, heads, HD)
    positions = jnp.concatenate([jnp.zeros((TXT, 3), jnp.float32), img_pos.astype(jnp.float32)], axis=0)
    cosine, sine = angles_of(positions, HD)
    query = rotate(rms_gain(mixed[:, :, 0], qk_gain[0]), cosine, sine).astype(jnp.bfloat16)
    keys = rotate(rms_gain(mixed[:, :, 1], qk_gain[1]), cosine, sine).astype(jnp.bfloat16)
    values = mixed[:, :, 2].astype(jnp.bfloat16)
    valid = key_valid(text_len, block_keep, seq_len)
    attention = lax.map(attend, (query, keys, values, valid))
    update = jnp.dot(attention.reshape(samples * seq_len, inner), w_out, preferred_element_type=jnp.float32)
    update = update.reshape(samples, seq_len, width) * mod_rows[:, 2]
    new_tokens = (tokens.astype(jnp.float32) + update).astype(jnp.bfloat16)
    text_out = new_tokens[:, :TXT]
    img_out = new_tokens[:, TXT:]
    final = modulate(img_out, mod_rows[:, 3], mod_rows[:, 4])
    velocity = jnp.dot(final.reshape(samples * IMG, width), w_final, preferred_element_type=jnp.float32)
    velocity = velocity.reshape(samples, IMG, w_final.shape[1])
    return (img_out, text_out, latent + step_size * velocity)
```

```python
import functools
import math

import jax
import jax.numpy as jnp
import numpy as np
from jax import lax
from jax.experimental import pallas as pl
from jax.experimental.pallas import tpu as pltpu
from jax.sharding import PartitionSpec as P

eps_norm = 1e-06
theta_base = 10000.0
step_size = -0.25
MIB = 1 << 20
F32 = jnp.float32
BF16 = jnp.bfloat16


def rope_rates(head_dim):
    half = head_dim // 2
    first = head_dim // 16
    second = (half - first) // 2
    counts = [first, second, half - first - second]
    tables = []
    for axis_id in range(3):
        pieces = []
        for other in range(3):
            if other == axis_id:
                pieces.append(theta_base ** (-np.arange(counts[other]) / counts[other]))
            else:
                pieces.append(np.zeros(counts[other]))
        tables.append(np.concatenate(pieces).astype(np.float32))
    return tables


def rope_tables(img_pos, text_rows, head_dim):
    tables = rope_rates(head_dim)
    pos = img_pos.astype(F32)
    angle = pos[:, 0:1] * tables[0] + pos[:, 1:2] * tables[1]
    angle = angle + pos[:, 2:3] * tables[2]
    half = head_dim // 2
    cosine = jnp.concatenate([jnp.ones((text_rows, half), F32), jnp.cos(angle)], axis=0)
    sine = jnp.concatenate([jnp.zeros((text_rows, half), F32), jnp.sin(angle)], axis=0)
    return (
        jnp.concatenate([cosine, cosine], axis=1),
        jnp.concatenate([-sine, sine], axis=1),
    )


def layer_norm(values):
    center = values - jnp.mean(values, axis=-1, keepdims=True)
    return center * lax.rsqrt(jnp.mean(center * center, axis=-1, keepdims=True) + eps_norm)


def norm_kernel(text_ref, img_ref, mod_ref, out_ref):
    s = pl.program_id(0)
    text_rows = text_ref.shape[1]
    shift = mod_ref[0, pl.ds(s, 1), :]
    scale = 1.0 + mod_ref[1, pl.ds(s, 1), :]
    out_ref[0, :text_rows] = (scale * layer_norm(text_ref[0].astype(F32)) + shift).astype(BF16)
    out_ref[0, text_rows:] = (scale * layer_norm(img_ref[0].astype(F32)) + shift).astype(BF16)


def norm_tokens(text_hidden, img_hidden, mod):
    samples, text_rows, width = text_hidden.shape
    img_rows = img_hidden.shape[1]
    rows = text_rows + img_rows
    return pl.pallas_call(
        norm_kernel,
        grid=(samples,),
        in_specs=[
            pl.BlockSpec((1, text_rows, width), lambda s: (s, 0, 0)),
            pl.BlockSpec((1, img_rows, width), lambda s: (s, 0, 0)),
            pl.BlockSpec((2, samples, width), lambda s: (0, 0, 0)),
        ],
        out_specs=pl.BlockSpec((1, rows, width), lambda s: (s, 0, 0)),
        out_shape=jax.ShapeDtypeStruct((samples, rows, width), BF16),
        compiler_params=pltpu.CompilerParams(vmem_limit_bytes=16 * MIB),
        cost_estimate=pl.CostEstimate(
            flops=samples * rows * width * 10,
            bytes_accessed=samples * rows * width * 4,
            transcendentals=0,
        ),
        name="norm_tokens",
    )(text_hidden, img_hidden, mod)


def qkv_kernel(col_ref, own_ref, other_ref, w_ref, rope_ref, gain_ref, out_ref):
    t = pl.program_id(1)
    samples, rows, width = own_ref.shape
    head_dim = gain_ref.shape[1]
    col = col_ref[0]

    def project(x_ref, half, place, rotated):
        y = jnp.dot(
            x_ref[...].reshape(samples * rows, width), w_ref[0], preferred_element_type=F32
        )
        for hh in range(2):
            v = y[:, hh * head_dim : (hh + 1) * head_dim]
            if rotated:
                v = v * lax.rsqrt(jnp.mean(v * v, axis=-1, keepdims=True) + eps_norm)
                v = v * gain_ref[pl.ds(t, 1), :]
                v3 = v.reshape(samples, rows, head_dim)
                r3 = pltpu.roll(v, head_dim // 2, 1).reshape(samples, rows, head_dim)
                v3 = v3 * rope_ref[half, 0][None] + r3 * rope_ref[half, 1][None]
            else:
                v3 = v.reshape(samples, rows, head_dim)
            out_ref[:, hh, place] = v3.astype(BF16)

    for half, x_ref in ((0, own_ref), (1, other_ref)):
        place = col if half == 0 else 1 - col

        @pl.when(t < 2)
        def _(x_ref=x_ref, half=half, place=place):
            project(x_ref, half, place, True)

        @pl.when(t == 2)
        def _(x_ref=x_ref, half=half, place=place):
            project(x_ref, half, place, False)


def qkv_heads(col, own, other, w_qkv, rope, gain, first, count):
    samples, rows, width = own.shape
    head_dim = gain.shape[1]
    return pl.pallas_call(
        qkv_kernel,
        grid_spec=pltpu.PrefetchScalarGridSpec(
            num_scalar_prefetch=1,
            grid=(count, 3),
            in_specs=[
                pl.BlockSpec((samples, rows, width), lambda j, t, c: (0, 0, 0)),
                pl.BlockSpec((samples, rows, width), lambda j, t, c: (0, 0, 0)),
                pl.BlockSpec((1, width, 2 * head_dim), lambda j, t, c: (t, 0, first + j)),
                pl.BlockSpec(rope.shape, lambda j, t, c: (0, 0, 0, 0)),
                pl.BlockSpec(gain.shape, lambda j, t, c: (0, 0)),
            ],
            out_specs=pl.BlockSpec(
                (samples, 2, 2, rows, head_dim), lambda j, t, c: (0, 0, 0, 0, 3 * j + t)
            ),
        ),
        out_shape=jax.ShapeDtypeStruct((samples, 2, 2, rows, 3 * count * head_dim), BF16),
        compiler_params=pltpu.CompilerParams(vmem_limit_bytes=32 * MIB),
        cost_estimate=pl.CostEstimate(
            flops=2 * samples * 2 * rows * width * 6 * count * head_dim,
            bytes_accessed=2 * (2 * samples * rows * width + width * 6 * count * head_dim),
            transcendentals=0,
        ),
        name="qkv_heads",
    )(col, own, other, w_qkv, rope, gain)


def attend_kernel(q_ref, k_ref, v_ref, bias_ref, *refs):
    out_ref = refs[-1]
    head_dim = q_ref.shape[1]
    factor = math.log2(math.e) / math.sqrt(head_dim)
    scores = lax.dot_general(
        q_ref[...], k_ref[...], (((1,), (1,)), ((), ())), preferred_element_type=F32
    )
    scores = scores * factor + bias_ref[...]
    top = jnp.max(scores, axis=-1, keepdims=True)
    weights = jnp.exp2(scores - top)
    total = jnp.sum(weights, axis=-1, keepdims=True)
    summed = jnp.dot(weights.astype(BF16), v_ref[...], preferred_element_type=F32)
    out_ref[...] = (summed / total).astype(BF16)


def attend(packed, bias, before, head_dim, block, first, heads):
    tokens = packed.shape[0]
    count = packed.shape[1] // (3 * head_dim)
    operands = [packed, packed, packed, bias]
    in_specs = [
        pl.BlockSpec((block, head_dim), lambda j, i: (i, 3 * j)),
        pl.BlockSpec((tokens, head_dim), lambda j, i: (0, 3 * j + 1)),
        pl.BlockSpec((tokens, head_dim), lambda j, i: (0, 3 * j + 2)),
        pl.BlockSpec((1, tokens), lambda j, i: (0, 0)),
    ]
    if before is not None:
        operands.append(before)
        in_specs.append(pl.BlockSpec(memory_space=pl.ANY))
    return pl.pallas_call(
        attend_kernel,
        grid=(count, tokens // block),
        in_specs=in_specs,
        out_specs=pl.BlockSpec((block, head_dim), lambda j, i: (i, first + j)),
        out_shape=jax.ShapeDtypeStruct((tokens, heads * head_dim), BF16),
        input_output_aliases={} if before is None else {4: 0},
        compiler_params=pltpu.CompilerParams(vmem_limit_bytes=32 * MIB),
        cost_estimate=pl.CostEstimate(
            flops=4 * count * tokens * tokens * head_dim,
            bytes_accessed=2 * 4 * count * tokens * head_dim,
            transcendentals=count * tokens * tokens,
        ),
        name="attend",
    )(*operands)


def finish_kernel(
    col_ref, att_ref, own_w_ref, other_w_ref, text_ref, img_ref, mod_ref, wf_ref,
    latent_ref, text_out_ref, img_out_ref, next_ref, acc, final
):
    hh = pl.program_id(0)
    side = pl.program_id(1)
    samples, text_rows, width = text_ref.shape
    img_rows = img_ref.shape[1]
    rows = text_rows + img_rows

    def add(w_ref):
        lhs = att_ref[...].reshape(samples * rows, att_ref.shape[-1])
        return jnp.dot(lhs, w_ref[...].reshape(-1, width), preferred_element_type=F32)

    @pl.when((hh == 0) & (side == 0))
    def _():
        acc[...] = add(own_w_ref)

    @pl.when((hh == 1) & (side == 0))
    def _():
        acc[...] += add(own_w_ref)

    @pl.when(side == 1)
    def _():
        acc[...] += add(other_w_ref)

    @pl.when((hh == 1) & (side == 1))
    def _():
        def sample(s, carry):
            start = pl.multiple_of(s * rows, 16)
            gate = mod_ref[2, pl.ds(s, 1), :]
            text_sum = acc[pl.ds(start, text_rows), :]
            text_out_ref[s] = (text_ref[s].astype(F32) + gate * text_sum).astype(BF16)
            img_sum = acc[pl.ds(start + text_rows, img_rows), :]
            img = (img_ref[s].astype(F32) + gate * img_sum).astype(BF16)
            img_out_ref[s] = img
            normed = layer_norm(img.astype(F32))
            scaled = (1.0 + mod_ref[4, pl.ds(s, 1), :]) * normed + mod_ref[3, pl.ds(s, 1), :]
            final[pl.ds(pl.multiple_of(s * img_rows, 16), img_rows), :] = scaled.astype(BF16)
            return carry

        lax.fori_loop(0, samples, sample, 0)
        velocity = lax.dot_general(
            final[...], wf_ref[...], (((1,), (1,)), ((), ())), preferred_element_type=F32
        )
        next_ref[...] = latent_ref[...] + step_size * velocity.reshape(latent_ref.shape)


def finish(col, att, own_w, other_w, text_hidden, img_hidden, mod, w_final, latent):
    samples, text_rows, width = text_hidden.shape
    img_rows = img_hidden.shape[1]
    rows = text_rows + img_rows
    groups = own_w.shape[0]
    head_dim = own_w.shape[2]
    whole = lambda shape: pl.BlockSpec(shape, lambda h, o, c: (0,) * len(shape))
    att_spec = pl.BlockSpec(
        (samples, None, None, rows, att.shape[-1]),
        lambda h, o, c: (0, h, c[0] + o - 2 * c[0] * o, 0, 0),
    )
    w_spec = pl.BlockSpec((groups, None, head_dim, width), lambda h, o, c: (0, h, 0, 0))
    return pl.pallas_call(
        finish_kernel,
        grid_spec=pltpu.PrefetchScalarGridSpec(
            num_scalar_prefetch=1,
            grid=(2, 2),
            in_specs=[
                att_spec,
                w_spec,
                w_spec,
                whole(text_hidden.shape),
                whole(img_hidden.shape),
                whole(mod.shape),
                whole(w_final.shape),
                whole(latent.shape),
            ],
            out_specs=[whole(text_hidden.shape), whole(img_hidden.shape), whole(latent.shape)],
            scratch_shapes=[
                pltpu.VMEM((samples * rows, width), F32),
                pltpu.VMEM((samples * img_rows, width), BF16),
            ],
        ),
        out_shape=[
            jax.ShapeDtypeStruct(text_hidden.shape, BF16),
            jax.ShapeDtypeStruct(img_hidden.shape, BF16),
            jax.ShapeDtypeStruct(latent.shape, F32),
        ],
        compiler_params=pltpu.CompilerParams(vmem_limit_bytes=48 * MIB),
        cost_estimate=pl.CostEstimate(
            flops=2 * samples * rows * width * groups * 4 * head_dim,
            bytes_accessed=4 * groups * 2 * head_dim * width * 2,
            transcendentals=0,
        ),
        name="finish",
    )(col, att, own_w, other_w, text_hidden, img_hidden, mod, w_final, latent)


def per_device(
    img_hidden,
    text_hidden,
    latent,
    text_len,
    block_keep,
    img_pos,
    modulation,
    qk_gain,
    w_qkv,
    w_out,
    w_final,
):
    samples, img_rows, width = img_hidden.shape
    text_rows = text_hidden.shape[1]
    rows = text_rows + img_rows
    head_dim = qk_gain.shape[1]
    groups = w_out.shape[0] // (2 * head_dim)
    tiles = lax.axis_size("row")
    swap = [(0, 1), (1, 0)]
    col = lax.axis_index("col").astype(jnp.int32).reshape(1)
    mod = jnp.transpose(modulation, (1, 0, 2))
    w_heads = jnp.transpose(w_qkv, (1, 0, 2))
    own_w = w_out.reshape(groups, 2, head_dim, width)

    other_pos = lax.ppermute(img_pos, "col", swap)
    normed = norm_tokens(text_hidden, img_hidden, mod)
    other_normed = lax.ppermute(normed, "col", swap)
    other_w = lax.ppermute(own_w, "col", swap)
    rope = jnp.stack(
        [
            jnp.stack(rope_tables(img_pos, text_rows, head_dim)),
            jnp.stack(rope_tables(other_pos, text_rows, head_dim)),
        ]
    )

    mine = lax.axis_index("row") // (tiles // samples)
    used = lax.dynamic_slice(text_len, (mine,), (1,))
    blocks = lax.dynamic_slice(block_keep, (mine, 0), (1, block_keep.shape[1]))
    text_at = jnp.arange(tiles * 2 * text_rows, dtype=jnp.int32).reshape(tiles, 2, text_rows)
    text_bias = jnp.where(text_at < used[0], 0.0, -1e30).astype(F32)
    img_bias = jnp.where(blocks[0][:, None, None] > 0, 0.0, -1e30).astype(F32)
    img_bias = jnp.broadcast_to(img_bias, (tiles, 2, img_rows))
    bias = jnp.concatenate([text_bias, img_bias], axis=2).reshape(1, tiles * 2 * rows)

    attention = None
    gathered = []
    for first, count in ((0, 1), (1, groups - 1)):
        mixed = qkv_heads(col, normed, other_normed, w_heads, rope, qk_gain, first, count)
        mixed = mixed.reshape(tiles, 2 * rows, 3 * count * head_dim)
        packed = lax.all_to_all(mixed, "row", 0, 0, tiled=True)
        gathered.append((first, packed.reshape(tiles * 2 * rows, 3 * count * head_dim)))
    for first, packed in gathered:
        attention = attend(packed, bias, attention, head_dim, 256, first, groups)
    attention = attention.reshape(tiles * 2, rows, groups * head_dim)
    back = lax.all_to_all(attention, ("row", "col"), 0, 0, tiled=True)
    back = back.reshape(samples, 2, 2, rows, groups * head_dim)
    text_out, img_out, latent_next = finish(
        col, back, own_w, other_w, text_hidden, img_hidden, mod, jnp.transpose(w_final), latent,
    )
    return (img_out, text_out, latent_next)


def solution(mesh):
    tokens = P("item", ("row", "col"), None)
    placed = (
        tokens,
        tokens,
        tokens,
        P("item"),
        P("item", None),
        P(("row", "col"), None),
        P("item", None, None),
        P(),
        P(None, None, "col"),
        P("col", None),
        P(),
    )
    return jax.shard_map(
        per_device,
        mesh=mesh,
        in_specs=placed,
        out_specs=(tokens, tokens, tokens),
        check_vma=False,
    )
```

```python
import functools
import math

import jax
import jax.numpy as jnp
import numpy as np
from jax import lax
from jax.experimental import pallas as pl
from jax.experimental.pallas import tpu as pltpu
from jax.sharding import PartitionSpec as P

eps_norm = 1e-06
theta_base = 10000.0
step_size = -0.25
excluded = -1e30
MIB = 1 << 20
F32 = jnp.float32
BF16 = jnp.bfloat16


def in_hbm(array):
    return pltpu.with_memory_space_constraint(array, pltpu.HBM)


def in_vmem():
    return pl.BlockSpec(memory_space=pltpu.VMEM)


def in_place():
    return pl.BlockSpec(memory_space=pl.ANY)


def rope_rates(head_dim):
    half = head_dim // 2
    first = head_dim // 16
    second = (half - first) // 2
    counts = [first, second, half - first - second]
    tables = []
    for axis_id in range(3):
        pieces = []
        for other in range(3):
            if other == axis_id:
                pieces.append(theta_base ** (-np.arange(counts[other]) / counts[other]))
            else:
                pieces.append(np.zeros(counts[other]))
        tables.append(np.concatenate(pieces + pieces).astype(np.float32))
    return np.stack(tables)


def layer_norm(values):
    center = values - jnp.mean(values, axis=-1, keepdims=True)
    return center * lax.rsqrt(jnp.mean(center * center, axis=-1, keepdims=True) + eps_norm)


def norm_kernel(text_ref, img_ref, mod_ref, out_ref):
    s = pl.program_id(0)
    text_rows = text_ref.shape[1]
    shift = mod_ref[0, pl.ds(s, 1), :]
    scale = 1.0 + mod_ref[1, pl.ds(s, 1), :]
    out_ref[0, :text_rows] = (scale * layer_norm(text_ref[0].astype(F32)) + shift).astype(BF16)
    out_ref[0, text_rows:] = (scale * layer_norm(img_ref[0].astype(F32)) + shift).astype(BF16)


def norm_tokens(text_hidden, img_hidden, mod):
    samples, text_rows, width = text_hidden.shape
    img_rows = img_hidden.shape[1]
    rows = text_rows + img_rows
    return pl.pallas_call(
        norm_kernel,
        grid=(samples,),
        in_specs=[
            pl.BlockSpec((1, text_rows, width), lambda s: (s, 0, 0)),
            pl.BlockSpec((1, img_rows, width), lambda s: (s, 0, 0)),
            pl.BlockSpec((2, samples, width), lambda s: (0, 0, 0)),
        ],
        out_specs=pl.BlockSpec((1, rows, width), lambda s: (s, 0, 0)),
        out_shape=jax.ShapeDtypeStruct((samples, rows, width), BF16),
        compiler_params=pltpu.CompilerParams(vmem_limit_bytes=16 * MIB),
        cost_estimate=pl.CostEstimate(
            flops=samples * rows * width * 10,
            bytes_accessed=samples * rows * width * 4,
            transcendentals=0,
        ),
        name="norm_tokens",
    )(in_hbm(text_hidden), in_hbm(img_hidden), in_hbm(mod))


def qkv_kernel(*refs, halves, first, count):
    x_refs, pos_refs = refs[: len(halves)], refs[len(halves) : 2 * len(halves)]
    w_hbm, rates_ref, gain_ref = refs[2 * len(halves) : 2 * len(halves) + 3]
    out_hbm, w_buf, stage, w_sems, out_sems = refs[-5:]
    samples, rows, width = x_refs[0].shape
    head_dim = gain_ref.shape[1]
    img_rows = pos_refs[0].shape[1]
    col = lax.axis_index("col")
    steps = [(j, t) for j in range(count) for t in range(3)]
    loads = []
    for n, (j, t) in enumerate(steps):
        columns = pl.ds((first + j) * 2 * head_dim, 2 * head_dim)
        loads.append(pltpu.make_async_copy(w_hbm.at[t, :, columns], w_buf.at[n], w_sems.at[n]))
        loads[-1].start()
    turns = []
    for pos_ref in pos_refs:
        angle = lax.dot_general(
            pos_ref[...].astype(F32), rates_ref[...], (((0,), (0,)), ((), ())),
            precision=lax.Precision.HIGHEST, preferred_element_type=F32,
        )
        angle = jnp.concatenate([jnp.zeros((rows - img_rows, head_dim), F32), angle], axis=0)
        lane = lax.broadcasted_iota(jnp.int32, angle.shape, 1)
        sine = jnp.sin(angle)
        turns.append((jnp.cos(angle), jnp.where(lane < head_dim // 2, -sine, sine)))
    stores = []
    for n, (j, t) in enumerate(steps):
        loads[n].wait()
        for h, x_ref in enumerate(x_refs):
            slot = n * len(halves) + h
            y = jnp.dot(
                x_ref[...].reshape(samples * rows, width), w_buf[n], preferred_element_type=F32
            )
            for hh in range(2):
                v = y[:, hh * head_dim : (hh + 1) * head_dim]
                if t < 2:
                    v = v * lax.rsqrt(jnp.mean(v * v, axis=-1, keepdims=True) + eps_norm)
                    v = v * gain_ref[t : t + 1, :]
                    rolled = pltpu.roll(v, head_dim // 2, 1).reshape(samples, rows, head_dim)
                    cosine, sine = turns[h]
                    v = v.reshape(samples, rows, head_dim) * cosine[None] + rolled * sine[None]
                stage[slot, :, hh] = v.reshape(samples, rows, head_dim).astype(BF16)
            place = col if halves[h] == 0 else 1 - col
            stores.append(
                pltpu.make_async_copy(
                    stage.at[slot], out_hbm.at[:, :, 3 * j + t, place], out_sems.at[slot]
                )
            )
            stores[-1].start()
    for store in stores:
        store.wait()


def qkv_heads(xs, positions, halves, w_qkv, gain, before, first, count):
    samples, rows, width = xs[0].shape
    head_dim = gain.shape[1]
    operands = [*xs, *positions, in_hbm(w_qkv), rope_rates(head_dim), gain]
    in_specs = [in_vmem() for _ in operands]
    in_specs[2 * len(xs)] = in_place()
    if before is not None:
        operands.append(in_hbm(before))
        in_specs.append(in_place())
    steps = 3 * count
    return pl.pallas_call(
        functools.partial(qkv_kernel, halves=halves, first=first, count=count),
        in_specs=in_specs,
        out_specs=in_place(),
        out_shape=pltpu.HBM((samples, 2, steps, 2, rows, head_dim), BF16),
        input_output_aliases={} if before is None else {len(operands) - 1: 0},
        scratch_shapes=[
            pltpu.VMEM((steps, width, 2 * head_dim), BF16),
            pltpu.VMEM((steps * len(xs), samples, 2, rows, head_dim), BF16),
            pltpu.SemaphoreType.DMA((steps,)),
            pltpu.SemaphoreType.DMA((steps * len(xs),)),
        ],
        compiler_params=pltpu.CompilerParams(vmem_limit_bytes=40 * MIB),
        cost_estimate=pl.CostEstimate(
            flops=2 * samples * len(xs) * rows * width * 2 * steps * head_dim,
            bytes_accessed=2 * (len(xs) * samples * rows * width + width * 2 * steps * head_dim),
            transcendentals=0,
        ),
        name="qkv_heads",
    )(*operands)


def attend_kernel(used_ref, keep_ref, q_ref, k_ref, v_ref, *refs, samples, text_rows, block):
    out_ref, wide_k, wide_v = refs[-3:]
    tiles, tile, head_dim = q_ref.shape
    tokens = tiles * tile
    rows = out_ref.shape[2]
    factor = math.log2(math.e) / math.sqrt(head_dim)

    @pl.when(pl.program_id(0) == 0)
    def _():
        mine = lax.axis_index("row") // (tiles // samples)
        used = used_ref[mine]
        at = lax.broadcasted_iota(jnp.int32, (tile, head_dim), 0)
        inner = at % rows
        text_at = (at // rows) * text_rows + inner
        for r in range(tiles):
            text_bias = jnp.where(text_at + r * 2 * text_rows < used, 0.0, excluded)
            img_bias = jnp.where(keep_ref[mine, r] > 0, 0.0, excluded)
            bias = jnp.where(inner < text_rows, text_bias, img_bias)
            wide_k[r * tile : (r + 1) * tile, head_dim:] = bias.astype(BF16)
        wide_v[:, head_dim:] = jnp.ones((tokens, head_dim), BF16)

    wide_k[:, :head_dim] = k_ref[...].reshape(tokens, head_dim)
    wide_v[:, :head_dim] = v_ref[...].reshape(tokens, head_dim)
    lane = lax.broadcasted_iota(jnp.int32, (block, head_dim), 1)
    one = jnp.where(lane == 0, 1.0, 0.0).astype(BF16)
    q = q_ref[...].reshape(tokens, head_dim)
    for m in range(0, tokens, block):
        wide_q = jnp.concatenate([q[m : m + block], one], axis=1)
        scores = lax.dot_general(
            wide_q, wide_k[...], (((1,), (1,)), ((), ())), preferred_element_type=F32
        )
        top = jnp.max(scores, axis=-1, keepdims=True)
        weights = jnp.exp2((scores - top) * factor).astype(BF16)
        summed = jnp.dot(weights, wide_v[...], preferred_element_type=F32)
        result = (summed[:, :head_dim] / summed[:, head_dim:]).astype(BF16)
        per = block // rows
        place = m // rows
        result = result.reshape(per, rows, head_dim)
        for p in range(per):
            out_ref[(place + p) // 2, (place + p) % 2] = result[p]


def attend(packed, text_len, block_keep, before, rows, text_rows, block, first, heads):
    tiles, steps, tile, head_dim = packed.shape
    count = steps // 3
    tokens = tiles * tile
    samples = text_len.shape[0]
    part = lambda t: pl.BlockSpec((tiles, None, tile, head_dim), lambda j: (0, 3 * j + t, 0, 0))
    smem = pl.BlockSpec(memory_space=pltpu.SMEM)
    operands = [text_len, block_keep, packed, packed, packed]
    in_specs = [smem, smem, part(0), part(1), part(2)]
    if before is not None:
        operands.append(in_hbm(before))
        in_specs.append(in_place())
    return pl.pallas_call(
        functools.partial(
            attend_kernel, samples=samples, text_rows=text_rows, block=block
        ),
        grid=(count,),
        in_specs=in_specs,
        out_specs=pl.BlockSpec(
            (tiles, 2, None, rows, head_dim), lambda j: (0, 0, first + j, 0, 0)
        ),
        out_shape=pltpu.HBM((tiles, 2, heads, rows, head_dim), BF16),
        input_output_aliases={} if before is None else {5: 0},
        scratch_shapes=[
            pltpu.VMEM((tokens, 2 * head_dim), BF16),
            pltpu.VMEM((tokens, 2 * head_dim), BF16),
        ],
        compiler_params=pltpu.CompilerParams(vmem_limit_bytes=40 * MIB),
        cost_estimate=pl.CostEstimate(
            flops=8 * count * tokens * tokens * head_dim,
            bytes_accessed=2 * 4 * count * tokens * head_dim,
            transcendentals=count * tokens * tokens,
        ),
        name="attend",
    )(*operands)


def finish_kernel(
    att_ref, own_w, other_w, text_hbm, img_hbm, mod_hbm, wf_hbm, latent_hbm,
    text_out_ref, img_out_ref, next_ref,
    w_buf, text, img, mod, wf, latent, acc, final, sems,
):
    samples, _, _, heads, rows, head_dim = att_ref.shape
    width = own_w.shape[-1]
    text_rows, img_rows = text.shape[1], img.shape[1]
    col = lax.axis_index("col")
    loads = []
    for hh in range(2):
        for k, (source, place) in enumerate(((own_w, col), (other_w, 1 - col))):
            loads.append(
                pltpu.make_async_copy(
                    source.at[:, hh], w_buf.at[hh, place], sems.at[2 * hh + k]
                )
            )
    others = [
        pltpu.make_async_copy(source, buf, sems.at[4 + k])
        for k, (source, buf) in enumerate(
            ((text_hbm, text), (img_hbm, img), (mod_hbm, mod), (wf_hbm, wf), (latent_hbm, latent))
        )
    ]
    for copy in loads + others:
        copy.start()

    def lhs(hh, low, high):
        pieces = [
            att_ref[low:high, hh, c, j].reshape((high - low) * rows, head_dim)
            for c in range(2)
            for j in range(heads)
        ]
        return jnp.concatenate(pieces, axis=1)

    def weight(hh):
        return w_buf[hh].reshape(2 * heads * head_dim, width)

    loads[0].wait()
    loads[1].wait()
    acc[...] = jnp.dot(lhs(0, 0, samples), weight(0), preferred_element_type=F32)
    loads[2].wait()
    loads[3].wait()
    for copy in others:
        copy.wait()
    group = samples // 2
    for low in range(0, samples, group):
        sums = acc[low * rows : (low + group) * rows]
        acc[low * rows : (low + group) * rows] = sums + jnp.dot(
            lhs(1, low, low + group), weight(1), preferred_element_type=F32
        )
        for s in range(low, low + group):
            gate = mod[2, s : s + 1, :]
            text_sum = acc[s * rows : s * rows + text_rows]
            text_out_ref[s] = (text[s].astype(F32) + gate * text_sum).astype(BF16)
            img_sum = acc[s * rows + text_rows : (s + 1) * rows]
            new_img = (img[s].astype(F32) + gate * img_sum).astype(BF16)
            img_out_ref[s] = new_img
            scaled = (1.0 + mod[4, s : s + 1, :]) * layer_norm(new_img.astype(F32))
            final[s * img_rows : (s + 1) * img_rows] = (scaled + mod[3, s : s + 1, :]).astype(BF16)
    velocity = lax.dot_general(
        final[...], wf[...], (((1,), (1,)), ((), ())), preferred_element_type=F32
    )
    next_ref[...] = latent[...] + step_size * velocity.reshape(latent.shape)


def finish(att, own_w, other_w, text_hidden, img_hidden, mod, w_final, latent):
    samples, text_rows, width = text_hidden.shape
    img_rows = img_hidden.shape[1]
    rows = text_rows + img_rows
    groups, _, head_dim, _ = own_w.shape
    return pl.pallas_call(
        finish_kernel,
        in_specs=[in_vmem()] + [in_place()] * 7,
        out_specs=[in_vmem()] * 3,
        out_shape=[
            pltpu.HBM(text_hidden.shape, BF16),
            pltpu.HBM(img_hidden.shape, BF16),
            pltpu.HBM(latent.shape, F32),
        ],
        scratch_shapes=[
            pltpu.VMEM((2, 2, groups, head_dim, width), BF16),
            pltpu.VMEM(text_hidden.shape, BF16),
            pltpu.VMEM(img_hidden.shape, BF16),
            pltpu.VMEM(mod.shape, F32),
            pltpu.VMEM(w_final.shape, BF16),
            pltpu.VMEM(latent.shape, F32),
            pltpu.VMEM((samples * rows, width), F32),
            pltpu.VMEM((samples * img_rows, width), BF16),
            pltpu.SemaphoreType.DMA((9,)),
        ],
        compiler_params=pltpu.CompilerParams(vmem_limit_bytes=48 * MIB),
        cost_estimate=pl.CostEstimate(
            flops=2 * samples * rows * width * groups * 4 * head_dim,
            bytes_accessed=4 * groups * 2 * head_dim * width * 2,
            transcendentals=0,
        ),
        name="finish",
    )(
        att, in_hbm(own_w), in_hbm(other_w), in_hbm(text_hidden), in_hbm(img_hidden),
        in_hbm(mod), in_hbm(w_final), in_hbm(latent),
    )


def per_device(
    img_hidden,
    text_hidden,
    latent,
    text_len,
    block_keep,
    img_pos,
    modulation,
    qk_gain,
    w_qkv,
    w_out,
    w_final,
):
    samples, img_rows, width = img_hidden.shape
    text_rows = text_hidden.shape[1]
    rows = text_rows + img_rows
    head_dim = qk_gain.shape[1]
    groups = w_out.shape[0] // (2 * head_dim)
    tiles = lax.axis_size("row")
    swap = [(0, 1), (1, 0)]
    mod = jnp.transpose(modulation, (1, 0, 2))
    w_heads = jnp.transpose(w_qkv, (1, 0, 2))
    own_w = w_out.reshape(groups, 2, head_dim, width)
    pos = jnp.transpose(img_pos)

    normed = norm_tokens(text_hidden, img_hidden, mod)
    other_normed = lax.ppermute(normed, "col", swap)
    other_pos = lax.ppermute(pos, "col", swap)
    other_w = lax.ppermute(own_w, "col", swap)

    def exchange(mixed):
        mixed = mixed.reshape(tiles, mixed.shape[2], 2 * rows, head_dim)
        return lax.all_to_all(mixed, "row", 0, 0, tiled=True)

    mixed = qkv_heads([normed], [pos], (0,), w_heads, qk_gain, None, 0, 1)
    mixed = qkv_heads([other_normed], [other_pos], (1,), w_heads, qk_gain, mixed, 0, 1)
    packed = exchange(mixed)
    late = qkv_heads(
        [normed, other_normed], [pos, other_pos], (0, 1), w_heads, qk_gain, None, 1, groups - 1
    )
    late = exchange(late)
    attention = attend(packed, text_len, block_keep, None, rows, text_rows, 384, 0, groups)
    attention = attend(late, text_len, block_keep, attention, rows, text_rows, 384, 1, groups)
    attention = attention.reshape(tiles * 2, groups, rows, head_dim)
    back = lax.all_to_all(attention, ("row", "col"), 0, 0, tiled=True)
    back = back.reshape(samples, 2, 2, groups, rows, head_dim)
    text_out, img_out, latent_next = finish(
        back, own_w, other_w, text_hidden, img_hidden, mod, jnp.transpose(w_final), latent
    )
    return (img_out, text_out, latent_next)


def solution(mesh):
    tokens = P("item", ("row", "col"), None)
    placed = (
        tokens,
        tokens,
        tokens,
        P("item"),
        P("item", None),
        P(("row", "col"), None),
        P("item", None, None),
        P(),
        P(None, None, "col"),
        P("col", None),
        P(),
    )
    return jax.shard_map(
        per_device,
        mesh=mesh,
        in_specs=placed,
        out_specs=(tokens, tokens, tokens),
        check_vma=False,
    )
```

```python
import functools
import math

import jax
import jax.numpy as jnp
import numpy as np
from jax import lax
from jax.experimental import pallas as pl
from jax.experimental.pallas import tpu as pltpu
from jax.sharding import PartitionSpec as P

eps_norm = 1e-06
theta_base = 10000.0
step_size = -0.25
excluded = -1e30
extra_rows = 16
MIB = 1 << 20
F32 = jnp.float32
BF16 = jnp.bfloat16


def in_hbm(array):
    return pltpu.with_memory_space_constraint(array, pltpu.HBM)


def in_vmem():
    return pl.BlockSpec(memory_space=pltpu.VMEM)


def in_place():
    return pl.BlockSpec(memory_space=pl.ANY)


def rope_rates(head_dim):
    half = head_dim // 2
    first = head_dim // 16
    second = (half - first) // 2
    counts = [first, second, half - first - second]
    tables = []
    for axis_id in range(3):
        pieces = []
        for other in range(3):
            if other == axis_id:
                pieces.append(theta_base ** (-np.arange(counts[other]) / counts[other]))
            else:
                pieces.append(np.zeros(counts[other]))
        tables.append(np.concatenate(pieces + pieces).astype(np.float32))
    tables += [np.zeros_like(tables[0])] * (8 - len(tables))
    return np.stack(tables)


def layer_norm(values):
    center = values - jnp.mean(values, axis=-1, keepdims=True)
    return center * lax.rsqrt(jnp.mean(center * center, axis=-1, keepdims=True) + eps_norm)


def norm_kernel(text_hbm, img_hbm, mod_hbm, w_hbm, pos_ref, out_ref, w_ref, text, img, mod, sems):
    samples, text_rows, _ = text.shape
    rows = text_rows + img.shape[1]
    columns = w_ref.shape[1] // 3
    mod_copy = pltpu.make_async_copy(mod_hbm.at[pl.ds(0, 2)], mod, sems.at[0])
    mod_copy.start()
    copies = []
    for s in range(samples):
        copies.append(
            (
                pltpu.make_async_copy(text_hbm.at[s], text.at[s], sems.at[1 + 2 * s]),
                pltpu.make_async_copy(img_hbm.at[s], img.at[s], sems.at[2 + 2 * s]),
            )
        )
        for copy in copies[-1]:
            copy.start()
    fetches = []
    for t in range(3):
        fetches.append(
            pltpu.make_async_copy(
                w_hbm.at[t, :, pl.ds(0, columns)],
                w_ref.at[:, pl.ds(t * columns, columns)],
                sems.at[1 + 2 * samples + t],
            )
        )
        fetches[-1].start()
    img_rows = pos_ref.shape[1]
    ids = jnp.zeros((extra_rows, img_rows), F32)
    row = lax.broadcasted_iota(jnp.int32, ids.shape, 0)
    for axis_id in range(pos_ref.shape[0]):
        ids = jnp.where(row == axis_id, pos_ref[axis_id : axis_id + 1, :].astype(F32), ids)
    out_ref[samples * rows :] = jnp.zeros((extra_rows, out_ref.shape[1]), BF16)
    out_ref[samples * rows :, :img_rows] = ids.astype(BF16)
    mod_copy.wait()
    for s in range(samples):
        for copy in copies[s]:
            copy.wait()
        shift = mod[0, s : s + 1, :]
        scale = 1.0 + mod[1, s : s + 1, :]
        begin, middle = s * rows, s * rows + text_rows
        text_norm = scale * layer_norm(text[s].astype(F32)) + shift
        out_ref[begin:middle] = text_norm.astype(BF16)
        img_norm = scale * layer_norm(img[s].astype(F32)) + shift
        out_ref[middle : begin + rows] = img_norm.astype(BF16)
    for fetch in fetches:
        fetch.wait()


def norm_tokens(text_hidden, img_hidden, mod, w_qkv, pos, head_dim):
    samples, text_rows, width = text_hidden.shape
    rows = text_rows + img_hidden.shape[1]
    return pl.pallas_call(
        norm_kernel,
        in_specs=[in_place()] * 4 + [in_vmem()],
        out_specs=[in_vmem(), in_vmem()],
        out_shape=[
            jax.ShapeDtypeStruct((samples * rows + extra_rows, width), BF16),
            jax.ShapeDtypeStruct((width, 6 * head_dim), BF16),
        ],
        scratch_shapes=[
            pltpu.VMEM(text_hidden.shape, BF16),
            pltpu.VMEM(img_hidden.shape, BF16),
            pltpu.VMEM((2, samples, width), F32),
            pltpu.SemaphoreType.DMA((4 + 2 * samples,)),
        ],
        compiler_params=pltpu.CompilerParams(vmem_limit_bytes=16 * MIB),
        cost_estimate=pl.CostEstimate(
            flops=samples * rows * width * 10,
            bytes_accessed=samples * rows * width * 4,
            transcendentals=0,
        ),
        name="norm_tokens",
    )(in_hbm(text_hidden), in_hbm(img_hidden), in_hbm(mod), in_hbm(w_qkv), pos)


def qkv_kernel(*refs, sides, jobs, ready, samples, img_rows):
    x_refs = refs[: len(sides)]
    w_hbm, rates_ref, gain_ref = refs[len(sides) : len(sides) + 3]
    out_hbm, w_buf, stage, w_sems, out_sems = refs[-5:]
    tokens = x_refs[0].shape[0] - extra_rows
    rows = tokens // samples
    head_dim = gain_ref.shape[1]
    col = lax.axis_index("col")
    wide = 2 * head_dim
    pairs = [pair for pair in sorted({job[1] for job in jobs}) if pair != ready]
    loads = {}
    for n, pair in enumerate(pairs):
        loads[pair] = [
            pltpu.make_async_copy(
                w_hbm.at[t, :, pl.ds(pair * wide, wide)],
                w_buf.at[n, :, pl.ds(t * wide, wide)],
                w_sems.at[3 * n + t],
            )
            for t in range(3)
        ]
        for load in loads[pair]:
            load.start()
    turns = []
    for x_ref in x_refs:
        ids = x_ref[tokens:, :128].astype(F32)[: rates_ref.shape[0], :img_rows]
        angle = lax.dot_general(
            ids, rates_ref[...], (((0,), (0,)), ((), ())),
            precision=lax.Precision.HIGHEST, preferred_element_type=F32,
        )
        angle = jnp.concatenate([jnp.zeros((rows - img_rows, head_dim), F32), angle], axis=0)
        lane = lax.broadcasted_iota(jnp.int32, angle.shape, 1)
        sine = jnp.sin(angle)
        turns.append((jnp.cos(angle), jnp.where(lane < head_dim // 2, -sine, sine)))
    stores = []
    for slot, (side, pair, base, placed) in enumerate(jobs):
        which = sides.index(side)
        if pair == ready:
            w_ref = refs[len(sides) + 3]
        else:
            w_ref = w_buf.at[pairs.index(pair)]
            for load in loads.pop(pair, []):
                load.wait()
        y = jnp.dot(x_refs[which][:tokens], w_ref[...], preferred_element_type=F32)
        cosine, sine = turns[which]
        for t in range(3):
            for hh in range(2):
                at = t * wide + hh * head_dim
                v = y[:, at : at + head_dim]
                if t < 2:
                    v = v * lax.rsqrt(jnp.mean(v * v, axis=-1, keepdims=True) + eps_norm)
                    v = v * gain_ref[t : t + 1, :]
                    rolled = pltpu.roll(v, head_dim // 2, 1).reshape(samples, rows, head_dim)
                    v = v.reshape(samples, rows, head_dim) * cosine[None] + rolled * sine[None]
                stage[slot, :, hh, t] = v.reshape(samples, rows, head_dim).astype(BF16)
        place = col if side == 0 else 1 - col
        begin = base + 3 * place if placed else base
        stores.append(
            pltpu.make_async_copy(
                stage.at[slot], out_hbm.at[:, :, pl.ds(begin, 3)], out_sems.at[slot]
            )
        )
        stores[-1].start()
    for store in stores:
        store.wait()


def qkv_heads(xs, sides, w_qkv, gain, samples, img_rows, first_w, jobs, slots, before=None):
    width = xs[0].shape[1]
    rows = (xs[0].shape[0] - extra_rows) // samples
    head_dim = gain.shape[1]
    operands = [*xs, in_hbm(w_qkv), rope_rates(head_dim), gain]
    in_specs = [in_vmem() for _ in operands]
    in_specs[len(xs)] = in_place()
    if first_w is not None:
        operands.append(first_w)
        in_specs.append(in_vmem())
    if before is not None:
        operands.append(in_hbm(before))
        in_specs.append(in_place())
    fetched = max(1, len({job[1] for job in jobs}) - (first_w is not None))
    return pl.pallas_call(
        functools.partial(
            qkv_kernel, sides=sides, jobs=jobs, samples=samples, img_rows=img_rows,
            ready=-1 if first_w is None else jobs[0][1],
        ),
        in_specs=in_specs,
        out_specs=in_place(),
        out_shape=pltpu.HBM((samples, 2, slots, rows, head_dim), BF16),
        input_output_aliases={} if before is None else {len(operands) - 1: 0},
        scratch_shapes=[
            pltpu.VMEM((fetched, width, 6 * head_dim), BF16),
            pltpu.VMEM((len(jobs), samples, 2, 3, rows, head_dim), BF16),
            pltpu.SemaphoreType.DMA((3 * fetched,)),
            pltpu.SemaphoreType.DMA((len(jobs),)),
        ],
        compiler_params=pltpu.CompilerParams(vmem_limit_bytes=24 * MIB),
        cost_estimate=pl.CostEstimate(
            flops=2 * samples * rows * width * 6 * len(jobs) * head_dim,
            bytes_accessed=2 * (len(xs) * samples * rows * width + width * 6 * head_dim),
            transcendentals=0,
        ),
        name="qkv_heads",
    )(*operands)


def attend_kernel(*refs, arrays, heads, samples, text_rows, step):
    used_ref, keep_ref = refs[:2]
    packed = refs[2 : 2 + arrays]
    out_hbm, wide_q, wide_k, wide_v, stage, sems = refs[-6:]
    tiles, _, rows, _ = wide_q.shape
    head_dim = packed[0].shape[-1]
    factor = math.log2(math.e) / math.sqrt(head_dim)
    col = lax.axis_index("col")
    mine = lax.axis_index("row") // (tiles // samples)
    used = used_ref[mine]
    at = lax.broadcasted_iota(jnp.int32, (rows, head_dim), 0)
    for r in range(tiles):
        img_bias = jnp.where(keep_ref[mine, r] > 0, 0.0, excluded)
        for half in range(2):
            text_at = at + (2 * r + half) * text_rows
            text_bias = jnp.where(text_at < used, 0.0, excluded)
            bias = jnp.where(at < text_rows, text_bias, img_bias)
            wide_k[r, half, :, head_dim:] = bias.astype(BF16)
    lane = lax.broadcasted_iota(jnp.int32, (tiles, 2, rows, head_dim), 3)
    wide_q[:, :, :, head_dim:] = jnp.where(lane == 0, 1.0, 0.0).astype(BF16)
    wide_v[:, :, :, head_dim:] = jnp.ones((tiles, 2, rows, head_dim), BF16)
    stores = []
    for n, (place, parts) in enumerate(heads):
        for array, slot, half in parts:
            half = col if half is None else 1 - col if half < 0 else half
            for t, wide in enumerate((wide_q, wide_k, wide_v)):
                wide[:, half, :, :head_dim] = packed[array][:, slot + t]
        keys = wide_k[...].reshape(tiles * 2 * rows, 2 * head_dim)
        values = wide_v[...].reshape(tiles * 2 * rows, 2 * head_dim)
        for r in range(0, tiles, step):
            scores = lax.dot_general(
                wide_q[r : r + step].reshape(step * 2 * rows, 2 * head_dim),
                keys,
                (((1,), (1,)), ((), ())),
                preferred_element_type=F32,
            )
            top = jnp.max(scores, axis=-1, keepdims=True)
            weights = jnp.exp2((scores - top) * factor).astype(BF16)
            summed = jnp.dot(weights, values, preferred_element_type=F32)
            result = (summed[:, :head_dim] / summed[:, head_dim:]).astype(BF16)
            stage[n, r : r + step] = result.reshape(step, 2, rows, head_dim)
        stores.append(pltpu.make_async_copy(stage.at[n], out_hbm.at[:, :, place], sems.at[n]))
        stores[-1].start()
    for store in stores:
        store.wait()


def attend(packed, heads, text_len, block_keep, before, text_rows, step, total):
    tiles, _, rows, head_dim = packed[0].shape
    tokens = tiles * 2 * rows
    samples = text_len.shape[0]
    smem = pl.BlockSpec(memory_space=pltpu.SMEM)
    operands = [text_len, block_keep, *packed]
    in_specs = [smem, smem] + [in_vmem()] * len(packed)
    if before is not None:
        operands.append(in_hbm(before))
        in_specs.append(in_place())
    return pl.pallas_call(
        functools.partial(
            attend_kernel, arrays=len(packed), heads=heads, samples=samples, text_rows=text_rows,
            step=step,
        ),
        in_specs=in_specs,
        out_specs=in_place(),
        out_shape=pltpu.HBM((tiles, 2, total, rows, head_dim), BF16),
        input_output_aliases={} if before is None else {len(operands) - 1: 0},
        scratch_shapes=[pltpu.VMEM((tiles, 2, rows, 2 * head_dim), BF16)] * 3
        + [
            pltpu.VMEM((len(heads), tiles, 2, rows, head_dim), BF16),
            pltpu.SemaphoreType.DMA((len(heads),)),
        ],
        compiler_params=pltpu.CompilerParams(vmem_limit_bytes=40 * MIB),
        cost_estimate=pl.CostEstimate(
            flops=8 * len(heads) * tokens * tokens * head_dim,
            bytes_accessed=2 * 4 * len(heads) * tokens * head_dim,
            transcendentals=len(heads) * tokens * tokens,
        ),
        name="attend",
    )(*operands)


def finish_kernel(
    att_ref, own_w, other_w, text, img, mod_hbm, wf_hbm, latent_hbm, text_hbm, img_hbm, next_ref,
    w_buf, mod, wf, latent, acc, final, text_new, img_new, sems,
):
    samples, _, _, heads, rows, head_dim = att_ref.shape
    width = own_w.shape[-1]
    text_rows, img_rows = text.shape[1], img.shape[1]
    col = lax.axis_index("col")
    one, rest = pl.ds(0, 1), pl.ds(1, heads - 1)
    loads = [
        (own_w.at[one], w_buf.at[0, one]),
        (own_w.at[rest], w_buf.at[0, rest]),
        (other_w, w_buf.at[1]),
        (mod_hbm, mod),
        (wf_hbm, wf),
        (latent_hbm, latent),
    ]
    loads = [pltpu.make_async_copy(a, b, sems.at[n]) for n, (a, b) in enumerate(loads)]
    for load in loads:
        load.start()

    def product(low, high, side, j_low, j_high):
        c = col if side == 0 else 1 - col
        pieces = [
            att_ref[low:high, hh, c, j].reshape((high - low) * rows, head_dim)
            for j in range(j_low, j_high)
            for hh in range(2)
        ]
        return jnp.dot(
            jnp.concatenate(pieces, axis=1),
            w_buf[side, j_low:j_high].reshape(2 * (j_high - j_low) * head_dim, width),
            preferred_element_type=F32,
        )

    loads[0].wait()
    acc[...] = product(0, samples, 0, 0, 1)
    loads[1].wait()
    acc[...] += product(0, samples, 0, 1, heads)
    for load in loads[2:]:
        load.wait()
    group = samples // 2
    stores = []
    for low in range(0, samples, group):
        acc[low * rows : (low + group) * rows] += product(low, low + group, 1, 0, heads)
        for s in range(low, low + group):
            gate = mod[2, s : s + 1, :]
            text_sum = acc[s * rows : s * rows + text_rows]
            text_new[s] = (text[s].astype(F32) + gate * text_sum).astype(BF16)
            img_sum = acc[s * rows + text_rows : (s + 1) * rows]
            new_img = (img[s].astype(F32) + gate * img_sum).astype(BF16)
            img_new[s] = new_img
            scaled = (1.0 + mod[4, s : s + 1, :]) * layer_norm(new_img.astype(F32))
            final[s * img_rows : (s + 1) * img_rows] = (scaled + mod[3, s : s + 1, :]).astype(BF16)
        part = pl.ds(low, group)
        for source, target in ((text_new, text_hbm), (img_new, img_hbm)):
            stores.append(
                pltpu.make_async_copy(
                    source.at[part], target.at[part], sems.at[len(loads) + len(stores)]
                )
            )
            stores[-1].start()
    velocity = lax.dot_general(
        final[...], wf[...], (((1,), (1,)), ((), ())), preferred_element_type=F32
    )
    next_ref[...] = latent[...] + step_size * velocity.reshape(latent.shape)
    for store in stores:
        store.wait()


def finish(att, own_w, other_w, text_hidden, img_hidden, mod, w_final, latent):
    samples, text_rows, width = text_hidden.shape
    img_rows = img_hidden.shape[1]
    rows = text_rows + img_rows
    near, far = in_vmem(), in_place()
    return pl.pallas_call(
        finish_kernel,
        in_specs=[near, far, far, near, near, far, far, far],
        out_specs=[far, far, near],
        out_shape=[
            pltpu.HBM(text_hidden.shape, BF16),
            pltpu.HBM(img_hidden.shape, BF16),
            pltpu.HBM(latent.shape, F32),
        ],
        scratch_shapes=[
            pltpu.VMEM((2, *own_w.shape), BF16),
            pltpu.VMEM(mod.shape, F32),
            pltpu.VMEM(w_final.shape, BF16),
            pltpu.VMEM(latent.shape, F32),
            pltpu.VMEM((samples * rows, width), F32),
            pltpu.VMEM((samples * img_rows, width), BF16),
            pltpu.VMEM(text_hidden.shape, BF16),
            pltpu.VMEM(img_hidden.shape, BF16),
            pltpu.SemaphoreType.DMA((10,)),
        ],
        compiler_params=pltpu.CompilerParams(vmem_limit_bytes=40 * MIB),
        cost_estimate=pl.CostEstimate(
            flops=4 * samples * rows * own_w.size,
            bytes_accessed=4 * own_w.size,
            transcendentals=0,
        ),
        name="finish",
    )(
        att, in_hbm(own_w), in_hbm(other_w), text_hidden, img_hidden, in_hbm(mod),
        in_hbm(w_final), in_hbm(latent),
    )


def per_device(
    img_hidden,
    text_hidden,
    latent,
    text_len,
    block_keep,
    img_pos,
    modulation,
    qk_gain,
    w_qkv,
    w_out,
    w_final,
):
    samples, img_rows, width = img_hidden.shape
    text_rows = text_hidden.shape[1]
    rows = text_rows + img_rows
    head_dim = qk_gain.shape[1]
    groups = w_out.shape[0] // (2 * head_dim)
    tiles = lax.axis_size("row")
    swap = [(0, 1), (1, 0)]
    mod = jnp.transpose(modulation, (1, 0, 2))
    w_heads = jnp.transpose(w_qkv, (1, 0, 2))
    own_w = w_out.reshape(groups, 2, head_dim, width)
    pos = jnp.transpose(img_pos)

    normed, first_w = norm_tokens(text_hidden, img_hidden, mod, w_heads, pos, head_dim)
    other_normed = lax.ppermute(normed, "col", swap)
    other_w = lax.ppermute(own_w, "col", swap)

    def exchange(mixed):
        mixed = mixed.reshape(tiles, mixed.shape[2], rows, head_dim)
        return lax.all_to_all(mixed, "row", 0, 0, tiled=True)

    sizes = (w_heads, qk_gain, samples, img_rows)
    both = ([normed, other_normed], (0, 1), *sizes)
    early = 1
    slots = 6 * early
    jobs = tuple((0, pair, 6 * pair, True) for pair in range(early))
    first = qkv_heads([normed], (0,), *sizes, first_w, jobs, slots)
    jobs = tuple((1, pair, 6 * pair, True) for pair in range(early))
    first = qkv_heads([other_normed], (1,), *sizes, first_w, jobs, slots, first)
    first = exchange(first)
    keys = (text_len, block_keep)

    def heads_of(low, high):
        return tuple((n, ((0, 6 * (n - low), 0), (0, 6 * (n - low) + 3, 1))) for n in range(low, high))

    jobs = tuple(
        (side, pair, 6 * (pair - early), True) for pair in range(early, groups) for side in range(2)
    )
    second = exchange(qkv_heads(*both, None, jobs, 6 * (groups - early)))
    attention = attend([first], heads_of(0, early), *keys, None, text_rows, 4, groups)
    attention = attend(
        [second], heads_of(early, groups), *keys, attention, text_rows, 4, groups
    )
    attention = attention.reshape(tiles * 2, groups, rows, head_dim)
    back = lax.all_to_all(attention, ("row", "col"), 0, 0, tiled=True)
    back = back.reshape(samples, 2, 2, groups, rows, head_dim)
    text_out, img_out, latent_next = finish(
        back, own_w, other_w, text_hidden, img_hidden, mod, jnp.transpose(w_final), latent
    )
    return (img_out, text_out, latent_next)


def solution(mesh):
    tokens = P("item", ("row", "col"), None)
    placed = (
        tokens,
        tokens,
        tokens,
        P("item"),
        P("item", None),
        P(("row", "col"), None),
        P("item", None, None),
        P(),
        P(None, None, "col"),
        P("col", None),
        P(),
    )
    return jax.shard_map(
        per_device,
        mesh=mesh,
        in_specs=placed,
        out_specs=(tokens, tokens, tokens),
        check_vma=False,
    )
```

```python
import functools
import math

import jax
import jax.numpy as jnp
import numpy as np
from jax import lax
from jax.experimental import pallas as pl
from jax.experimental.pallas import tpu as pltpu
from jax.sharding import PartitionSpec as P

eps_norm = 1e-06
theta_base = 10000.0
step_size = -0.25
excluded = -1e30
extra_rows = 16
MIB = 1 << 20
F32 = jnp.float32
BF16 = jnp.bfloat16


def in_hbm(array):
    return pltpu.with_memory_space_constraint(array, pltpu.HBM)


def in_vmem():
    return pl.BlockSpec(memory_space=pltpu.VMEM)


def in_place():
    return pl.BlockSpec(memory_space=pl.ANY)


def rope_rates(head_dim):
    half = head_dim // 2
    first = head_dim // 16
    second = (half - first) // 2
    counts = [first, second, half - first - second]
    tables = []
    for axis_id in range(3):
        pieces = []
        for other in range(3):
            if other == axis_id:
                pieces.append(theta_base ** (-np.arange(counts[other]) / counts[other]))
            else:
                pieces.append(np.zeros(counts[other]))
        tables.append(np.concatenate(pieces + pieces).astype(np.float32))
    tables += [np.zeros_like(tables[0])] * (8 - len(tables))
    return np.stack(tables)


def layer_norm(values):
    center = values - jnp.mean(values, axis=-1, keepdims=True)
    return center * lax.rsqrt(jnp.mean(center * center, axis=-1, keepdims=True) + eps_norm)


def norm_kernel(
    text_hbm, img_hbm, mod_hbm, w_hbm, pos_hbm, out_ref, w_ref, text, img, mod, pos_ref, sems
):
    samples, text_rows, _ = text.shape
    rows = text_rows + img.shape[1]
    columns = w_ref.shape[1] // 3
    mod_copy = pltpu.make_async_copy(mod_hbm.at[pl.ds(0, 2)], mod, sems.at[0])
    mod_copy.start()
    pos_copy = pltpu.make_async_copy(pos_hbm, pos_ref, sems.at[4 + 2 * samples])
    pos_copy.start()
    copies = []
    for s in range(samples):
        copies.append(
            (
                pltpu.make_async_copy(text_hbm.at[s], text.at[s], sems.at[1 + 2 * s]),
                pltpu.make_async_copy(img_hbm.at[s], img.at[s], sems.at[2 + 2 * s]),
            )
        )
        for copy in copies[-1]:
            copy.start()
    fetches = []
    for t in range(3):
        fetches.append(
            pltpu.make_async_copy(
                w_hbm.at[t, :, pl.ds(0, columns)],
                w_ref.at[:, pl.ds(t * columns, columns)],
                sems.at[1 + 2 * samples + t],
            )
        )
        fetches[-1].start()
    mod_copy.wait()
    for s in range(samples):
        for copy in copies[s]:
            copy.wait()
        shift = mod[0, s : s + 1, :]
        scale = 1.0 + mod[1, s : s + 1, :]
        begin, middle = s * rows, s * rows + text_rows
        text_norm = scale * layer_norm(text[s].astype(F32)) + shift
        out_ref[begin:middle] = text_norm.astype(BF16)
        img_norm = scale * layer_norm(img[s].astype(F32)) + shift
        out_ref[middle : begin + rows] = img_norm.astype(BF16)
    pos_copy.wait()
    img_rows = pos_ref.shape[1]
    ids = jnp.zeros((extra_rows, img_rows), F32)
    row = lax.broadcasted_iota(jnp.int32, ids.shape, 0)
    for axis_id in range(pos_ref.shape[0]):
        ids = jnp.where(row == axis_id, pos_ref[axis_id : axis_id + 1, :].astype(F32), ids)
    out_ref[samples * rows :] = jnp.zeros((extra_rows, out_ref.shape[1]), BF16)
    out_ref[samples * rows :, :img_rows] = ids.astype(BF16)
    for fetch in fetches:
        fetch.wait()


def norm_tokens(text_hidden, img_hidden, mod, w_qkv, pos, head_dim):
    samples, text_rows, width = text_hidden.shape
    rows = text_rows + img_hidden.shape[1]
    return pl.pallas_call(
        norm_kernel,
        in_specs=[in_place()] * 5,
        out_specs=[in_vmem(), in_vmem()],
        out_shape=[
            jax.ShapeDtypeStruct((samples * rows + extra_rows, width), BF16),
            jax.ShapeDtypeStruct((width, 6 * head_dim), BF16),
        ],
        scratch_shapes=[
            pltpu.VMEM(text_hidden.shape, BF16),
            pltpu.VMEM(img_hidden.shape, BF16),
            pltpu.VMEM((2, samples, width), F32),
            pltpu.VMEM(pos.shape, jnp.int32),
            pltpu.SemaphoreType.DMA((5 + 2 * samples,)),
        ],
        compiler_params=pltpu.CompilerParams(vmem_limit_bytes=16 * MIB),
        cost_estimate=pl.CostEstimate(
            flops=samples * rows * width * 10,
            bytes_accessed=samples * rows * width * 4,
            transcendentals=0,
        ),
        name="norm_tokens",
    )(in_hbm(text_hidden), in_hbm(img_hidden), in_hbm(mod), in_hbm(w_qkv), in_hbm(pos))


def qkv_kernel(*refs, sides, jobs, ready, samples, img_rows):
    x_refs = refs[: len(sides)]
    w_hbm, rates_ref, gain_ref = refs[len(sides) : len(sides) + 3]
    out_hbm, w_buf, stage, w_sems, out_sems = refs[-5:]
    tokens = x_refs[0].shape[0] - extra_rows
    rows = tokens // samples
    head_dim = gain_ref.shape[1]
    col = lax.axis_index("col")
    wide = 2 * head_dim
    pairs = [pair for pair in sorted({job[1] for job in jobs}) if pair != ready]
    loads = {}
    for n, pair in enumerate(pairs):
        loads[pair] = [
            pltpu.make_async_copy(
                w_hbm.at[t, :, pl.ds(pair * wide, wide)],
                w_buf.at[n, :, pl.ds(t * wide, wide)],
                w_sems.at[3 * n + t],
            )
            for t in range(3)
        ]
        for load in loads[pair]:
            load.start()
    turns = []
    for x_ref in x_refs:
        ids = x_ref[tokens:, :128].astype(F32)[: rates_ref.shape[0], :img_rows]
        angle = lax.dot_general(
            ids, rates_ref[...], (((0,), (0,)), ((), ())),
            precision=lax.Precision.HIGHEST, preferred_element_type=F32,
        )
        angle = jnp.concatenate([jnp.zeros((rows - img_rows, head_dim), F32), angle], axis=0)
        lane = lax.broadcasted_iota(jnp.int32, angle.shape, 1)
        sine = jnp.sin(angle)
        turns.append((jnp.cos(angle), jnp.where(lane < head_dim // 2, -sine, sine)))
    stores = []
    for slot, (side, pair, base, placed) in enumerate(jobs):
        which = sides.index(side)
        if pair == ready:
            w_ref = refs[len(sides) + 3]
        else:
            w_ref = w_buf.at[pairs.index(pair)]
            for load in loads.pop(pair, []):
                load.wait()
        y = jnp.dot(x_refs[which][:tokens], w_ref[...], preferred_element_type=F32)
        cosine, sine = turns[which]
        place = col if side == 0 else 1 - col
        begin = base + 3 * place if placed else base
        for t in range(3):
            for hh in range(2):
                at = t * wide + hh * head_dim
                v = y[:, at : at + head_dim]
                if t < 2:
                    v = v * lax.rsqrt(jnp.mean(v * v, axis=-1, keepdims=True) + eps_norm)
                    v = v * gain_ref[t : t + 1, :]
                    rolled = pltpu.roll(v, head_dim // 2, 1).reshape(samples, rows, head_dim)
                    v = v.reshape(samples, rows, head_dim) * cosine[None] + rolled * sine[None]
                stage[slot, t, :, hh] = v.reshape(samples, rows, head_dim).astype(BF16)
            stores.append(
                pltpu.make_async_copy(
                    stage.at[slot, t], out_hbm.at[:, :, begin + t], out_sems.at[3 * slot + t]
                )
            )
            stores[-1].start()
    for store in stores:
        store.wait()


def qkv_heads(xs, sides, w_qkv, gain, samples, img_rows, first_w, jobs, slots, before=None):
    width = xs[0].shape[1]
    rows = (xs[0].shape[0] - extra_rows) // samples
    head_dim = gain.shape[1]
    operands = [*xs, in_hbm(w_qkv), rope_rates(head_dim), gain]
    in_specs = [in_vmem() for _ in operands]
    in_specs[len(xs)] = in_place()
    if first_w is not None:
        operands.append(first_w)
        in_specs.append(in_vmem())
    if before is not None:
        operands.append(in_hbm(before))
        in_specs.append(in_place())
    fetched = max(1, len({job[1] for job in jobs}) - (first_w is not None))
    return pl.pallas_call(
        functools.partial(
            qkv_kernel, sides=sides, jobs=jobs, samples=samples, img_rows=img_rows,
            ready=-1 if first_w is None else jobs[0][1],
        ),
        in_specs=in_specs,
        out_specs=in_place(),
        out_shape=pltpu.HBM((samples, 2, slots, rows, head_dim), BF16),
        input_output_aliases={} if before is None else {len(operands) - 1: 0},
        scratch_shapes=[
            pltpu.VMEM((fetched, width, 6 * head_dim), BF16),
            pltpu.VMEM((len(jobs), 3, samples, 2, rows, head_dim), BF16),
            pltpu.SemaphoreType.DMA((3 * fetched,)),
            pltpu.SemaphoreType.DMA((3 * len(jobs),)),
        ],
        compiler_params=pltpu.CompilerParams(vmem_limit_bytes=24 * MIB),
        cost_estimate=pl.CostEstimate(
            flops=2 * samples * rows * width * 6 * len(jobs) * head_dim,
            bytes_accessed=2 * (len(xs) * samples * rows * width + width * 6 * head_dim),
            transcendentals=0,
        ),
        name="qkv_heads",
    )(*operands)


def attend_kernel(*refs, arrays, heads, samples, text_rows, step):
    used_ref, keep_ref = refs[:2]
    packed = refs[2 : 2 + arrays]
    out_hbm, wide_q, wide_k, wide_v, all_scores, stage, sems = refs[-7:]
    tiles, _, rows, _ = wide_q.shape
    head_dim = packed[0].shape[-1]
    factor = math.log2(math.e) / math.sqrt(head_dim)
    mine = lax.axis_index("row") // (tiles // samples)
    used = used_ref[mine]
    at = lax.broadcasted_iota(jnp.int32, (rows, head_dim), 0)
    for r in range(tiles):
        img_bias = jnp.where(keep_ref[mine, r] > 0, 0.0, excluded)
        for half in range(2):
            text_at = at + (2 * r + half) * text_rows
            text_bias = jnp.where(text_at < used, 0.0, excluded)
            bias = jnp.where(at < text_rows, text_bias, img_bias)
            wide_k[r, half, :, head_dim:] = bias.astype(BF16)
    lane = lax.broadcasted_iota(jnp.int32, (tiles, 2, rows, head_dim), 3)
    wide_q[:, :, :, head_dim:] = jnp.where(lane == 0, 1.0, 0.0).astype(BF16)
    wide_v[:, :, :, head_dim:] = jnp.ones((tiles, 2, rows, head_dim), BF16)
    stores = []
    for n, (place, parts) in enumerate(heads):
        for array, slot, half in parts:
            for t, wide in enumerate((wide_q, wide_k, wide_v)):
                wide[:, half, :, :head_dim] = packed[array][:, slot + t]
        all_scores[...] = lax.dot_general(
            wide_q[...].reshape(tiles * 2 * rows, 2 * head_dim),
            wide_k[...].reshape(tiles * 2 * rows, 2 * head_dim),
            (((1,), (1,)), ((), ())),
            preferred_element_type=F32,
        )
        values = wide_v[...].reshape(tiles * 2 * rows, 2 * head_dim)
        for r in range(0, tiles, step):
            scores = all_scores[r * 2 * rows : (r + step) * 2 * rows]
            top = jnp.max(scores, axis=-1, keepdims=True)
            weights = jnp.exp2((scores - top) * factor).astype(BF16)
            summed = jnp.dot(weights, values, preferred_element_type=F32)
            result = (summed[:, :head_dim] / summed[:, head_dim:]).astype(BF16)
            stage[n, r : r + step] = result.reshape(step, 2, rows, head_dim)
        stores.append(pltpu.make_async_copy(stage.at[n], out_hbm.at[:, :, place], sems.at[n]))
        stores[-1].start()
    for store in stores:
        store.wait()


def attend(packed, heads, text_len, block_keep, before, text_rows, step, total):
    tiles, _, rows, head_dim = packed[0].shape
    tokens = tiles * 2 * rows
    samples = text_len.shape[0]
    smem = pl.BlockSpec(memory_space=pltpu.SMEM)
    operands = [text_len, block_keep, *packed]
    in_specs = [smem, smem] + [in_vmem()] * len(packed)
    if before is not None:
        operands.append(in_hbm(before))
        in_specs.append(in_place())
    return pl.pallas_call(
        functools.partial(
            attend_kernel, arrays=len(packed), heads=heads, samples=samples, text_rows=text_rows,
            step=step,
        ),
        in_specs=in_specs,
        out_specs=in_place(),
        out_shape=pltpu.HBM((tiles, 2, total, rows, head_dim), BF16),
        input_output_aliases={} if before is None else {len(operands) - 1: 0},
        scratch_shapes=[pltpu.VMEM((tiles, 2, rows, 2 * head_dim), BF16)] * 3
        + [
            pltpu.VMEM((tokens, tokens), F32),
            pltpu.VMEM((len(heads), tiles, 2, rows, head_dim), BF16),
            pltpu.SemaphoreType.DMA((len(heads),)),
        ],
        compiler_params=pltpu.CompilerParams(vmem_limit_bytes=40 * MIB),
        cost_estimate=pl.CostEstimate(
            flops=8 * len(heads) * tokens * tokens * head_dim,
            bytes_accessed=2 * 4 * len(heads) * tokens * head_dim,
            transcendentals=len(heads) * tokens * tokens,
        ),
        name="attend",
    )(*operands)


def finish_kernel(
    att_ref, own_w, other_w, text, img, mod_hbm, wf_hbm, latent_hbm, text_hbm, img_hbm, next_ref,
    w_buf, mod, wf, latent, acc, final, text_new, img_new, sems,
):
    samples, _, _, heads, rows, head_dim = att_ref.shape
    width = own_w.shape[-1]
    text_rows, img_rows = text.shape[1], img.shape[1]
    col = lax.axis_index("col")
    one, rest = pl.ds(0, 1), pl.ds(1, heads - 1)
    loads = [
        (own_w.at[one], w_buf.at[0, one]),
        (own_w.at[rest], w_buf.at[0, rest]),
        (other_w, w_buf.at[1]),
        (mod_hbm, mod),
        (wf_hbm, wf),
        (latent_hbm, latent),
    ]
    loads = [pltpu.make_async_copy(a, b, sems.at[n]) for n, (a, b) in enumerate(loads)]
    for load in loads:
        load.start()

    def product(low, high, side, j_low, j_high):
        c = col if side == 0 else 1 - col
        pieces = [
            att_ref[low:high, hh, c, j].reshape((high - low) * rows, head_dim)
            for j in range(j_low, j_high)
            for hh in range(2)
        ]
        return jnp.dot(
            jnp.concatenate(pieces, axis=1),
            w_buf[side, j_low:j_high].reshape(2 * (j_high - j_low) * head_dim, width),
            preferred_element_type=F32,
        )

    loads[0].wait()
    acc[...] = product(0, samples, 0, 0, 1)
    loads[1].wait()
    acc[...] += product(0, samples, 0, 1, heads)
    for load in loads[2:]:
        load.wait()
    group = samples // 2
    stores = []
    for low in range(0, samples, group):
        acc[low * rows : (low + group) * rows] += product(low, low + group, 1, 0, heads)
        for s in range(low, low + group):
            gate = mod[2, s : s + 1, :]
            text_sum = acc[s * rows : s * rows + text_rows]
            text_new[s] = (text[s].astype(F32) + gate * text_sum).astype(BF16)
            img_sum = acc[s * rows + text_rows : (s + 1) * rows]
            new_img = (img[s].astype(F32) + gate * img_sum).astype(BF16)
            img_new[s] = new_img
            scaled = (1.0 + mod[4, s : s + 1, :]) * layer_norm(new_img.astype(F32))
            final[s * img_rows : (s + 1) * img_rows] = (scaled + mod[3, s : s + 1, :]).astype(BF16)
        part = pl.ds(low, group)
        for source, target in ((text_new, text_hbm), (img_new, img_hbm)):
            stores.append(
                pltpu.make_async_copy(
                    source.at[part], target.at[part], sems.at[len(loads) + len(stores)]
                )
            )
            stores[-1].start()
    velocity = lax.dot_general(
        final[...], wf[...], (((1,), (1,)), ((), ())), preferred_element_type=F32
    )
    next_ref[...] = latent[...] + step_size * velocity.reshape(latent.shape)
    for store in stores:
        store.wait()


def finish(att, own_w, other_w, text_hidden, img_hidden, mod, w_final, latent):
    samples, text_rows, width = text_hidden.shape
    img_rows = img_hidden.shape[1]
    rows = text_rows + img_rows
    near, far = in_vmem(), in_place()
    return pl.pallas_call(
        finish_kernel,
        in_specs=[near, far, far, near, near, far, far, far],
        out_specs=[far, far, near],
        out_shape=[
            pltpu.HBM(text_hidden.shape, BF16),
            pltpu.HBM(img_hidden.shape, BF16),
            pltpu.HBM(latent.shape, F32),
        ],
        scratch_shapes=[
            pltpu.VMEM((2, *own_w.shape), BF16),
            pltpu.VMEM(mod.shape, F32),
            pltpu.VMEM(w_final.shape, BF16),
            pltpu.VMEM(latent.shape, F32),
            pltpu.VMEM((samples * rows, width), F32),
            pltpu.VMEM((samples * img_rows, width), BF16),
            pltpu.VMEM(text_hidden.shape, BF16),
            pltpu.VMEM(img_hidden.shape, BF16),
            pltpu.SemaphoreType.DMA((10,)),
        ],
        compiler_params=pltpu.CompilerParams(vmem_limit_bytes=40 * MIB),
        cost_estimate=pl.CostEstimate(
            flops=4 * samples * rows * own_w.size,
            bytes_accessed=4 * own_w.size,
            transcendentals=0,
        ),
        name="finish",
    )(
        att, in_hbm(own_w), in_hbm(other_w), text_hidden, img_hidden, in_hbm(mod),
        in_hbm(w_final), in_hbm(latent),
    )


def per_device(
    img_hidden,
    text_hidden,
    latent,
    text_len,
    block_keep,
    img_pos,
    modulation,
    qk_gain,
    w_qkv,
    w_out,
    w_final,
):
    samples, img_rows, width = img_hidden.shape
    text_rows = text_hidden.shape[1]
    rows = text_rows + img_rows
    head_dim = qk_gain.shape[1]
    groups = w_out.shape[0] // (2 * head_dim)
    tiles = lax.axis_size("row")
    swap = [(0, 1), (1, 0)]
    mod = jnp.transpose(modulation, (1, 0, 2))
    w_heads = jnp.transpose(w_qkv, (1, 0, 2))
    own_w = w_out.reshape(groups, 2, head_dim, width)
    pos = jnp.transpose(img_pos)

    normed, first_w = norm_tokens(text_hidden, img_hidden, mod, w_heads, pos, head_dim)
    other_normed = lax.ppermute(normed, "col", swap)
    other_w = lax.ppermute(own_w, "col", swap)

    def exchange(mixed):
        mixed = mixed.reshape(tiles, mixed.shape[2], rows, head_dim)
        return lax.all_to_all(mixed, "row", 0, 0, tiled=True)

    sizes = (w_heads, qk_gain, samples, img_rows)
    both = ([normed, other_normed], (0, 1), *sizes)
    early = 1
    slots = 6 * early
    jobs = tuple((0, pair, 6 * pair, True) for pair in range(early))
    first = qkv_heads([normed], (0,), *sizes, first_w, jobs, slots)
    jobs = tuple((1, pair, 6 * pair, True) for pair in range(early))
    first = qkv_heads([other_normed], (1,), *sizes, first_w, jobs, slots, first)
    first = exchange(first)
    keys = (text_len, block_keep)

    def heads_of(low, high):
        return tuple((n, ((0, 6 * (n - low), 0), (0, 6 * (n - low) + 3, 1))) for n in range(low, high))

    jobs = tuple(
        (side, pair, 6 * (pair - early), True) for pair in range(early, groups) for side in range(2)
    )
    second = exchange(qkv_heads(*both, None, jobs, 6 * (groups - early)))
    attention = attend([first], heads_of(0, early), *keys, None, text_rows, 4, groups)
    attention = attend(
        [second], heads_of(early, groups), *keys, attention, text_rows, 4, groups
    )
    attention = attention.reshape(tiles * 2, groups, rows, head_dim)
    back = lax.all_to_all(attention, ("row", "col"), 0, 0, tiled=True)
    back = back.reshape(samples, 2, 2, groups, rows, head_dim)
    text_out, img_out, latent_next = finish(
        back, own_w, other_w, text_hidden, img_hidden, mod, jnp.transpose(w_final), latent
    )
    return (img_out, text_out, latent_next)


def solution(mesh):
    tokens = P("item", ("row", "col"), None)
    placed = (
        tokens,
        tokens,
        tokens,
        P("item"),
        P("item", None),
        P(("row", "col"), None),
        P("item", None, None),
        P(),
        P(None, None, "col"),
        P("col", None),
        P(),
    )
    return jax.shard_map(
        per_device,
        mesh=mesh,
        in_specs=placed,
        out_specs=(tokens, tokens, tokens),
        check_vma=False,
    )
```

```python
import functools
import math

import jax
import jax.numpy as jnp
import numpy as np
from jax import lax
from jax.experimental import pallas as pl
from jax.experimental.pallas import tpu as pltpu
from jax.sharding import PartitionSpec as P

eps_norm = 1e-06
theta_base = 10000.0
step_size = -0.25
excluded = -1e30
extra_rows = 16
MIB = 1 << 20
F32 = jnp.float32
BF16 = jnp.bfloat16


def in_hbm(array):
    return pltpu.with_memory_space_constraint(array, pltpu.HBM)


def in_vmem():
    return pl.BlockSpec(memory_space=pltpu.VMEM)


def in_place():
    return pl.BlockSpec(memory_space=pl.ANY)


def rope_rates(head_dim):
    half = head_dim // 2
    first = head_dim // 16
    second = (half - first) // 2
    counts = [first, second, half - first - second]
    tables = []
    for axis_id in range(3):
        pieces = []
        for other in range(3):
            if other == axis_id:
                pieces.append(theta_base ** (-np.arange(counts[other]) / counts[other]))
            else:
                pieces.append(np.zeros(counts[other]))
        tables.append(np.concatenate(pieces + pieces).astype(np.float32))
    tables += [np.zeros_like(tables[0])] * (8 - len(tables))
    return np.stack(tables)


def layer_norm(values):
    center = values - jnp.mean(values, axis=-1, keepdims=True)
    return center * lax.rsqrt(jnp.mean(center * center, axis=-1, keepdims=True) + eps_norm)


def norm_kernel(
    text_hbm, img_hbm, mod_hbm, w_hbm, pos_hbm, out_ref, w_ref, text, img, mod, pos_ref, sems
):
    samples, text_rows, _ = text.shape
    rows = text_rows + img.shape[1]
    columns = w_ref.shape[1] // 3
    mod_copy = pltpu.make_async_copy(mod_hbm.at[pl.ds(0, 2)], mod, sems.at[0])
    mod_copy.start()
    pos_copy = pltpu.make_async_copy(pos_hbm, pos_ref, sems.at[4 + 2 * samples])
    pos_copy.start()
    copies = []
    for s in range(samples):
        copies.append(
            (
                pltpu.make_async_copy(text_hbm.at[s], text.at[s], sems.at[1 + 2 * s]),
                pltpu.make_async_copy(img_hbm.at[s], img.at[s], sems.at[2 + 2 * s]),
            )
        )
        for copy in copies[-1]:
            copy.start()
    fetches = []
    for t in range(3):
        fetches.append(
            pltpu.make_async_copy(
                w_hbm.at[t, :, pl.ds(0, columns)],
                w_ref.at[:, pl.ds(t * columns, columns)],
                sems.at[1 + 2 * samples + t],
            )
        )
        fetches[-1].start()
    mod_copy.wait()
    for s in range(samples):
        for copy in copies[s]:
            copy.wait()
        shift = mod[0, s : s + 1, :]
        scale = 1.0 + mod[1, s : s + 1, :]
        begin, middle = s * rows, s * rows + text_rows
        text_norm = scale * layer_norm(text[s].astype(F32)) + shift
        out_ref[begin:middle] = text_norm.astype(BF16)
        img_norm = scale * layer_norm(img[s].astype(F32)) + shift
        out_ref[middle : begin + rows] = img_norm.astype(BF16)
    pos_copy.wait()
    img_rows = pos_ref.shape[1]
    ids = jnp.zeros((extra_rows, img_rows), F32)
    row = lax.broadcasted_iota(jnp.int32, ids.shape, 0)
    for axis_id in range(pos_ref.shape[0]):
        ids = jnp.where(row == axis_id, pos_ref[axis_id : axis_id + 1, :].astype(F32), ids)
    out_ref[samples * rows :] = jnp.zeros((extra_rows, out_ref.shape[1]), BF16)
    out_ref[samples * rows :, :img_rows] = ids.astype(BF16)
    for fetch in fetches:
        fetch.wait()


def norm_tokens(text_hidden, img_hidden, mod, w_qkv, pos, head_dim):
    samples, text_rows, width = text_hidden.shape
    rows = text_rows + img_hidden.shape[1]
    return pl.pallas_call(
        norm_kernel,
        in_specs=[in_place()] * 5,
        out_specs=[in_vmem(), in_vmem()],
        out_shape=[
            jax.ShapeDtypeStruct((samples * rows + extra_rows, width), BF16),
            jax.ShapeDtypeStruct((width, 6 * head_dim), BF16),
        ],
        scratch_shapes=[
            pltpu.VMEM(text_hidden.shape, BF16),
            pltpu.VMEM(img_hidden.shape, BF16),
            pltpu.VMEM((2, samples, width), F32),
            pltpu.VMEM(pos.shape, jnp.int32),
            pltpu.SemaphoreType.DMA((5 + 2 * samples,)),
        ],
        compiler_params=pltpu.CompilerParams(vmem_limit_bytes=16 * MIB),
        cost_estimate=pl.CostEstimate(
            flops=samples * rows * width * 10,
            bytes_accessed=samples * rows * width * 4,
            transcendentals=0,
        ),
        name="norm_tokens",
    )(in_hbm(text_hidden), in_hbm(img_hidden), in_hbm(mod), in_hbm(w_qkv), in_hbm(pos))


def qkv_kernel(*refs, sides, jobs, ready, samples, img_rows):
    x_refs = refs[: len(sides)]
    w_hbm, rates_ref, gain_ref = refs[len(sides) : len(sides) + 3]
    out_hbm, w_buf, stage, w_sems, out_sems = refs[-5:]
    tokens = x_refs[0].shape[0] - extra_rows
    rows = tokens // samples
    head_dim = gain_ref.shape[1]
    col = lax.axis_index("col")
    wide = 2 * head_dim
    pairs = [pair for pair in sorted({job[1] for job in jobs}) if pair != ready]
    loads = {}
    for n, pair in enumerate(pairs):
        loads[pair] = [
            pltpu.make_async_copy(
                w_hbm.at[t, :, pl.ds(pair * wide, wide)],
                w_buf.at[n, :, pl.ds(t * wide, wide)],
                w_sems.at[3 * n + t],
            )
            for t in range(3)
        ]
        for load in loads[pair]:
            load.start()
    turns = []
    for x_ref in x_refs:
        ids = x_ref[tokens:, :128].astype(F32)[: rates_ref.shape[0], :img_rows]
        angle = lax.dot_general(
            ids, rates_ref[...], (((0,), (0,)), ((), ())),
            precision=lax.Precision.HIGHEST, preferred_element_type=F32,
        )
        angle = jnp.concatenate([jnp.zeros((rows - img_rows, head_dim), F32), angle], axis=0)
        lane = lax.broadcasted_iota(jnp.int32, angle.shape, 1)
        sine = jnp.sin(angle)
        turns.append((jnp.cos(angle), jnp.where(lane < head_dim // 2, -sine, sine)))
    stores = []
    for slot, (side, pair, base, placed) in enumerate(jobs):
        which = sides.index(side)
        if pair == ready:
            w_ref = refs[len(sides) + 3]
        else:
            w_ref = w_buf.at[pairs.index(pair)]
            for load in loads.pop(pair, []):
                load.wait()
        y = jnp.dot(x_refs[which][:tokens], w_ref[...], preferred_element_type=F32)
        cosine, sine = turns[which]
        place = col if side == 0 else 1 - col
        begin = base + 3 * place if placed else base
        for t in range(3):
            for hh in range(2):
                at = t * wide + hh * head_dim
                v = y[:, at : at + head_dim]
                if t < 2:
                    v = v * lax.rsqrt(jnp.mean(v * v, axis=-1, keepdims=True) + eps_norm)
                    v = v * gain_ref[t : t + 1, :]
                    rolled = pltpu.roll(v, head_dim // 2, 1).reshape(samples, rows, head_dim)
                    v = v.reshape(samples, rows, head_dim) * cosine[None] + rolled * sine[None]
                stage[slot, t, :, hh] = v.reshape(samples, rows, head_dim).astype(BF16)
            stores.append(
                pltpu.make_async_copy(
                    stage.at[slot, t], out_hbm.at[:, :, begin + t], out_sems.at[3 * slot + t]
                )
            )
            stores[-1].start()
    for store in stores:
        store.wait()


def qkv_heads(xs, sides, w_qkv, gain, samples, img_rows, first_w, jobs, slots, before=None):
    width = xs[0].shape[1]
    rows = (xs[0].shape[0] - extra_rows) // samples
    head_dim = gain.shape[1]
    operands = [*xs, in_hbm(w_qkv), rope_rates(head_dim), gain]
    in_specs = [in_vmem() for _ in operands]
    in_specs[len(xs)] = in_place()
    if first_w is not None:
        operands.append(first_w)
        in_specs.append(in_vmem())
    if before is not None:
        operands.append(in_hbm(before))
        in_specs.append(in_place())
    fetched = max(1, len({job[1] for job in jobs}) - (first_w is not None))
    return pl.pallas_call(
        functools.partial(
            qkv_kernel, sides=sides, jobs=jobs, samples=samples, img_rows=img_rows,
            ready=-1 if first_w is None else jobs[0][1],
        ),
        in_specs=in_specs,
        out_specs=in_place(),
        out_shape=pltpu.HBM((samples, 2, slots, rows, head_dim), BF16),
        input_output_aliases={} if before is None else {len(operands) - 1: 0},
        scratch_shapes=[
            pltpu.VMEM((fetched, width, 6 * head_dim), BF16),
            pltpu.VMEM((len(jobs), 3, samples, 2, rows, head_dim), BF16),
            pltpu.SemaphoreType.DMA((3 * fetched,)),
            pltpu.SemaphoreType.DMA((3 * len(jobs),)),
        ],
        compiler_params=pltpu.CompilerParams(vmem_limit_bytes=24 * MIB),
        cost_estimate=pl.CostEstimate(
            flops=2 * samples * rows * width * 6 * len(jobs) * head_dim,
            bytes_accessed=2 * (len(xs) * samples * rows * width + width * 6 * head_dim),
            transcendentals=0,
        ),
        name="qkv_heads",
    )(*operands)


def attend_kernel(*refs, arrays, heads, samples, text_rows, step):
    used_ref, keep_ref = refs[:2]
    packed = refs[2 : 2 + arrays]
    out_hbm, wide_q, wide_k, wide_v, all_scores, stage, sems = refs[-7:]
    tiles, _, rows, _ = wide_q.shape
    head_dim = packed[0].shape[-1]
    factor = math.log2(math.e) / math.sqrt(head_dim)
    mine = lax.axis_index("row") // (tiles // samples)
    used = used_ref[mine]
    at = lax.broadcasted_iota(jnp.int32, (rows, head_dim), 0)
    for r in range(tiles):
        img_bias = jnp.where(keep_ref[mine, r] > 0, 0.0, excluded)
        for half in range(2):
            text_at = at + (2 * r + half) * text_rows
            text_bias = jnp.where(text_at < used, 0.0, excluded)
            bias = jnp.where(at < text_rows, text_bias, img_bias)
            wide_k[r, half, :, head_dim:] = bias.astype(BF16)
    lane = lax.broadcasted_iota(jnp.int32, (tiles, 2, rows, head_dim), 3)
    wide_q[:, :, :, head_dim:] = jnp.where(lane == 0, 1.0, 0.0).astype(BF16)
    wide_v[:, :, :, head_dim:] = jnp.ones((tiles, 2, rows, head_dim), BF16)
    stores = []
    for n, (place, parts) in enumerate(heads):
        for array, slot, half in parts:
            for t, wide in enumerate((wide_q, wide_k, wide_v)):
                wide[:, half, :, :head_dim] = packed[array][:, slot + t]
        all_scores[...] = lax.dot_general(
            wide_q[...].reshape(tiles * 2 * rows, 2 * head_dim),
            wide_k[...].reshape(tiles * 2 * rows, 2 * head_dim),
            (((1,), (1,)), ((), ())),
            preferred_element_type=F32,
        )
        values = wide_v[...].reshape(tiles * 2 * rows, 2 * head_dim)
        for r in range(0, tiles, step):
            scores = all_scores[r * 2 * rows : (r + step) * 2 * rows]
            top = jnp.max(scores, axis=-1, keepdims=True)
            weights = jnp.exp2((scores - top) * factor).astype(BF16)
            summed = jnp.dot(weights, values, preferred_element_type=F32)
            result = (summed[:, :head_dim] / summed[:, head_dim:]).astype(BF16)
            stage[n, r : r + step] = result.reshape(step, 2, rows, head_dim)
        stores.append(pltpu.make_async_copy(stage.at[n], out_hbm.at[:, :, place], sems.at[n]))
        stores[-1].start()
    for store in stores:
        store.wait()


def attend(packed, heads, text_len, block_keep, before, text_rows, step, total):
    tiles, _, rows, head_dim = packed[0].shape
    tokens = tiles * 2 * rows
    samples = text_len.shape[0]
    smem = pl.BlockSpec(memory_space=pltpu.SMEM)
    operands = [text_len, block_keep, *packed]
    in_specs = [smem, smem] + [in_vmem()] * len(packed)
    if before is not None:
        operands.append(in_hbm(before))
        in_specs.append(in_place())
    return pl.pallas_call(
        functools.partial(
            attend_kernel, arrays=len(packed), heads=heads, samples=samples, text_rows=text_rows,
            step=step,
        ),
        in_specs=in_specs,
        out_specs=in_place(),
        out_shape=pltpu.HBM((tiles, 2, total, rows, head_dim), BF16),
        input_output_aliases={} if before is None else {len(operands) - 1: 0},
        scratch_shapes=[pltpu.VMEM((tiles, 2, rows, 2 * head_dim), BF16)] * 3
        + [
            pltpu.VMEM((tokens, tokens), F32),
            pltpu.VMEM((len(heads), tiles, 2, rows, head_dim), BF16),
            pltpu.SemaphoreType.DMA((len(heads),)),
        ],
        compiler_params=pltpu.CompilerParams(vmem_limit_bytes=40 * MIB),
        cost_estimate=pl.CostEstimate(
            flops=8 * len(heads) * tokens * tokens * head_dim,
            bytes_accessed=2 * 4 * len(heads) * tokens * head_dim,
            transcendentals=len(heads) * tokens * tokens,
        ),
        name="attend",
    )(*operands)


def finish_kernel(
    att_ref, own_w, other_w, text, img, mod_hbm, wf_hbm, latent_hbm, text_hbm, img_hbm, next_ref,
    w_buf, mod, wf, latent, acc, final, text_new, img_new, sems,
):
    samples, _, _, heads, rows, head_dim = att_ref.shape
    width = own_w.shape[-1]
    text_rows, img_rows = text.shape[1], img.shape[1]
    col = lax.axis_index("col")
    loads = [
        (own_w, w_buf.at[0]),
        (other_w, w_buf.at[1]),
        (mod_hbm, mod),
        (wf_hbm, wf),
        (latent_hbm, latent),
    ]
    loads = [pltpu.make_async_copy(a, b, sems.at[n]) for n, (a, b) in enumerate(loads)]
    for load in loads:
        load.start()

    def product(low, high, side, j_low, j_high):
        c = col if side == 0 else 1 - col
        pieces = [
            att_ref[low:high, hh, c, j].reshape((high - low) * rows, head_dim)
            for j in range(j_low, j_high)
            for hh in range(2)
        ]
        return jnp.dot(
            jnp.concatenate(pieces, axis=1),
            w_buf[side, j_low:j_high].reshape(2 * (j_high - j_low) * head_dim, width),
            preferred_element_type=F32,
        )

    loads[0].wait()
    acc[...] = product(0, samples, 0, 0, heads)
    for load in loads[1:]:
        load.wait()
    group = samples // 2
    stores = []
    for low in range(0, samples, group):
        acc[low * rows : (low + group) * rows] += product(low, low + group, 1, 0, heads)
        for s in range(low, low + group):
            gate = mod[2, s : s + 1, :]
            text_sum = acc[s * rows : s * rows + text_rows]
            text_new[s] = (text[s].astype(F32) + gate * text_sum).astype(BF16)
            img_sum = acc[s * rows + text_rows : (s + 1) * rows]
            new_img = (img[s].astype(F32) + gate * img_sum).astype(BF16)
            img_new[s] = new_img
            scaled = (1.0 + mod[4, s : s + 1, :]) * layer_norm(new_img.astype(F32))
            final[s * img_rows : (s + 1) * img_rows] = (scaled + mod[3, s : s + 1, :]).astype(BF16)
        part = pl.ds(low, group)
        for source, target in ((text_new, text_hbm), (img_new, img_hbm)):
            stores.append(
                pltpu.make_async_copy(
                    source.at[part], target.at[part], sems.at[len(loads) + len(stores)]
                )
            )
            stores[-1].start()
    velocity = lax.dot_general(
        final[...], wf[...], (((1,), (1,)), ((), ())), preferred_element_type=F32
    )
    next_ref[...] = latent[...] + step_size * velocity.reshape(latent.shape)
    for store in stores:
        store.wait()


def finish(att, own_w, other_w, text_hidden, img_hidden, mod, w_final, latent):
    samples, text_rows, width = text_hidden.shape
    img_rows = img_hidden.shape[1]
    rows = text_rows + img_rows
    near, far = in_vmem(), in_place()
    return pl.pallas_call(
        finish_kernel,
        in_specs=[near, far, far, near, near, far, far, far],
        out_specs=[far, far, near],
        out_shape=[
            pltpu.HBM(text_hidden.shape, BF16),
            pltpu.HBM(img_hidden.shape, BF16),
            pltpu.HBM(latent.shape, F32),
        ],
        scratch_shapes=[
            pltpu.VMEM((2, *own_w.shape), BF16),
            pltpu.VMEM(mod.shape, F32),
            pltpu.VMEM(w_final.shape, BF16),
            pltpu.VMEM(latent.shape, F32),
            pltpu.VMEM((samples * rows, width), F32),
            pltpu.VMEM((samples * img_rows, width), BF16),
            pltpu.VMEM(text_hidden.shape, BF16),
            pltpu.VMEM(img_hidden.shape, BF16),
            pltpu.SemaphoreType.DMA((10,)),
        ],
        compiler_params=pltpu.CompilerParams(vmem_limit_bytes=40 * MIB),
        cost_estimate=pl.CostEstimate(
            flops=4 * samples * rows * own_w.size,
            bytes_accessed=4 * own_w.size,
            transcendentals=0,
        ),
        name="finish",
    )(
        att, in_hbm(own_w), in_hbm(other_w), text_hidden, img_hidden, in_hbm(mod),
        in_hbm(w_final), in_hbm(latent),
    )


def per_device(
    img_hidden,
    text_hidden,
    latent,
    text_len,
    block_keep,
    img_pos,
    modulation,
    qk_gain,
    w_qkv,
    w_out,
    w_final,
):
    samples, img_rows, width = img_hidden.shape
    text_rows = text_hidden.shape[1]
    rows = text_rows + img_rows
    head_dim = qk_gain.shape[1]
    groups = w_out.shape[0] // (2 * head_dim)
    tiles = lax.axis_size("row")
    swap = [(0, 1), (1, 0)]
    mod = jnp.transpose(modulation, (1, 0, 2))
    w_heads = jnp.transpose(w_qkv, (1, 0, 2))
    own_w = w_out.reshape(groups, 2, head_dim, width)
    pos = jnp.transpose(img_pos)

    normed, first_w = norm_tokens(text_hidden, img_hidden, mod, w_heads, pos, head_dim)
    other_normed = lax.ppermute(normed, "col", swap)
    other_w = lax.ppermute(own_w, "col", swap)

    def exchange(mixed):
        mixed = mixed.reshape(tiles, mixed.shape[2], rows, head_dim)
        return lax.all_to_all(mixed, "row", 0, 0, tiled=True)

    sizes = (w_heads, qk_gain, samples, img_rows)
    both = ([normed, other_normed], (0, 1), *sizes)
    early = 1
    slots = 6 * early
    jobs = tuple((0, pair, 6 * pair, True) for pair in range(early))
    first = qkv_heads([normed], (0,), *sizes, first_w, jobs, slots)
    jobs = tuple((1, pair, 6 * pair, True) for pair in range(early))
    first = qkv_heads([other_normed], (1,), *sizes, first_w, jobs, slots, first)
    first = exchange(first)
    keys = (text_len, block_keep)

    def heads_of(low, high):
        return tuple((n, ((0, 6 * (n - low), 0), (0, 6 * (n - low) + 3, 1))) for n in range(low, high))

    jobs = tuple(
        (side, pair, 6 * (pair - early), True) for pair in range(early, groups) for side in range(2)
    )
    second = exchange(qkv_heads(*both, None, jobs, 6 * (groups - early)))
    attention = attend([first], heads_of(0, early), *keys, None, text_rows, 8, groups)
    attention = attend(
        [second], heads_of(early, groups), *keys, attention, text_rows, 8, groups
    )
    attention = attention.reshape(tiles * 2, groups, rows, head_dim)
    back = lax.all_to_all(attention, ("row", "col"), 0, 0, tiled=True)
    back = back.reshape(samples, 2, 2, groups, rows, head_dim)
    text_out, img_out, latent_next = finish(
        back, own_w, other_w, text_hidden, img_hidden, mod, jnp.transpose(w_final), latent
    )
    return (img_out, text_out, latent_next)


def solution(mesh):
    tokens = P("item", ("row", "col"), None)
    placed = (
        tokens,
        tokens,
        tokens,
        P("item"),
        P("item", None),
        P(("row", "col"), None),
        P("item", None, None),
        P(),
        P(None, None, "col"),
        P("col", None),
        P(),
    )
    return jax.shard_map(
        per_device,
        mesh=mesh,
        in_specs=placed,
        out_specs=(tokens, tokens, tokens),
        check_vma=False,
    )
```
